512 devices in a mesh: rad: 64 (over z, y), col: 8 (over x, core).
Axes of the slice: x: 4, y: 8, z: 8, core: 2. Of those that a mesh axis runs over, the one named last changes fastest.
Arguments:
- right_sides: bfloat16 [256, 384, 1024], P('rad', None, 'col'), may hold values from -6 to 6
- coarse_solution: bfloat16 [64, 384, 1024], P('rad', None, 'col'), may hold values from -6 to 6
- lift_one: bfloat16 [128, 2, 1024, 1024], P('rad', None, 'col'), may hold values from -0.125 to 0.125
- solve_one: bfloat16 [128, 3, 1024, 1024], P('rad', None, 'col'), may hold values from -0.109375 to 0.109375
- lift_two: bfloat16 [64, 2, 1024, 1024], P('rad', None, 'col'), may hold values from -0.125 to 0.125
- solve_two: bfloat16 [64, 3, 1024, 1024], P('rad', None, 'col'), may hold values from -0.109375 to 0.109375
Outputs:
- solution: bfloat16 [256, 384, 1024], P('rad', None, 'col')
- reduced_sides: bfloat16 [64, 384, 1024], P('rad', None, 'col')
The draws below stay inside these ranges and needn't reach their ends.
All inputs are finite; a program needn't handle non-finite values.
Results may differ from the reference program's by a relative error of at most 0.007.
Values may be sent and summed in bfloat16 or wider, within the bound.
No kernel may reach another device: no remote copies, remote signals or barrier semaphores. Data moves between devices by JAX's collectives and lax.ppermute only.
A program may use at most 64 MiB of HBM per device.

```python
import jax
import jax.numpy as jnp
from jax import lax

CHANNELS = 1024
VECTORS = 384
BLOCKS = 256
GROUPS = 64


def level_of(rng, extent, shards, least, high):
    def one(axis_at, blocks):
        heights = jax.random.uniform(jax.random.fold_in(jax.random.fold_in(rng, 6), axis_at), (blocks,), jnp.float32, least / len(shards), high / len(shards))
        return jnp.repeat(jnp.exp(heights), extent[axis_at] // blocks).reshape((-1,) + (1,) * (len(extent) - axis_at - 1))

    factor_of = one(*shards[0])
    for cut in shards[1:]:
        factor_of = factor_of * one(*cut)
    return factor_of


def centred(stream_key, dims, spread, most, split=(), held_as=jnp.bfloat16):
    drawn = jax.random.normal(stream_key, dims, jnp.float32) * spread
    if len(split) > 0:
        drawn = level_of(stream_key, dims, split, -0.22, 0.18) * drawn
    return jnp.clip(drawn, min=-most, max=most).astype(held_as)


def setup_inputs(seed: int = 0) -> dict:
    seeds = jax.random.split(jax.random.key(seed), 7)
    return {
        "right_sides": centred(seeds[0], (BLOCKS, VECTORS, CHANNELS), 1.0, 6.0, ((0, 64), (2, 8))),
        "coarse_solution": centred(seeds[1], (GROUPS, VECTORS, CHANNELS), 1.0, 6.0, ((0, 64), (2, 8))),
        "lift_one": centred(seeds[2], (BLOCKS // 2, 2, CHANNELS, CHANNELS), (2 * CHANNELS) ** -0.5, 0.125, ((0, 64), (2, 8))),
        "solve_one": centred(seeds[3], (BLOCKS // 2, 3, CHANNELS, CHANNELS), (3 * CHANNELS) ** -0.5, 0.109375, ((0, 64), (2, 8))),
        "lift_two": centred(seeds[4], (GROUPS, 2, CHANNELS, CHANNELS), (2 * CHANNELS) ** -0.5, 0.125, ((0, 64), (2, 8))),
        "solve_two": centred(seeds[5], (GROUPS, 3, CHANNELS, CHANNELS), (3 * CHANNELS) ** -0.5, 0.109375, ((0, 64), (2, 8))),
    }


def apply(vector, matrix):
    return jnp.dot(vector, matrix.T, preferred_element_type=jnp.float32)


def level_one(inputs):
    quartet, before, lift = inputs
    first = quartet[0].astype(jnp.float32) - apply(before, lift[0, 0]) - apply(quartet[1], lift[0, 1])
    third = quartet[2].astype(jnp.float32) - apply(quartet[1], lift[1, 0]) - apply(quartet[3], lift[1, 1])
    return first.astype(jnp.bfloat16), third.astype(jnp.bfloat16)


def level_two(inputs):
    kept, middle, middle_before, quartet, lift_pair, solve_pair, solve_triple, coarse_here, coarse_next = inputs
    reduced = kept.astype(jnp.float32) - apply(middle_before, lift_pair[0]) - apply(middle, lift_pair[1])
    centre = apply(middle, solve_triple[0]) - apply(coarse_here, solve_triple[1]) - apply(coarse_next, solve_triple[2])
    centre = centre.astype(jnp.bfloat16)
    second = apply(quartet[1], solve_pair[0, 0]) - apply(coarse_here, solve_pair[0, 1]) - apply(centre, solve_pair[0, 2])
    fourth = apply(quartet[3], solve_pair[1, 0]) - apply(centre, solve_pair[1, 1]) - apply(coarse_next, solve_pair[1, 2])
    stacked = jnp.stack([coarse_here, second.astype(jnp.bfloat16), centre, fourth.astype(jnp.bfloat16)])
    return reduced.astype(jnp.bfloat16), stacked


def reference(right_sides, coarse_solution, lift_one, solve_one, lift_two, solve_two):
    groups = BLOCKS // 4
    quartets = right_sides.reshape(groups, 4, VECTORS, CHANNELS)
    zero_block = jnp.zeros((1, VECTORS, CHANNELS), right_sides.dtype)
    before = jnp.concatenate([zero_block, quartets[:-1, 3]], axis=0)
    after = jnp.concatenate([coarse_solution[1:], zero_block], axis=0)
    lift_groups = lift_one.reshape(groups, 2, 2, CHANNELS, CHANNELS)
    kept, middle = lax.map(level_one, (quartets, before, lift_groups))
    middle_before = jnp.concatenate([zero_block, middle[:-1]], axis=0)
    solve_groups = solve_one.reshape(groups, 2, 3, CHANNELS, CHANNELS)
    reduced, solved = lax.map(level_two, (kept, middle, middle_before, quartets, lift_two, solve_groups, solve_two, coarse_solution, after))
    return solved.reshape(BLOCKS, VECTORS, CHANNELS), reduced
```

```python
import functools

import jax
import jax.numpy as jnp
from jax import lax
from jax.experimental import pallas as pl
from jax.experimental.pallas import tpu as pltpu
from jax.sharding import PartitionSpec as P

ROWS = 384
WIDTH = 128
BF16 = jnp.bfloat16
F32 = jnp.float32


def chips_of(peers):
    return [[i for i in range(peers) if i % 2 == core] for core in range(2)]


def cores_of(peers):
    return [[i, i + 1] for i in range(0, peers, 2)]


def over_chips(array):
    peers = lax.axis_size("col")
    chips = peers // 2
    copies = jnp.broadcast_to(array[None], (chips, *array.shape))
    return lax.all_to_all(copies, "col", 0, 0, axis_index_groups=chips_of(peers))


def over_cores(array):
    peers = lax.axis_size("col")
    return lax.all_gather(array, "col", axis=0, axis_index_groups=cores_of(peers))


def passed_along(array, by):
    peers = lax.axis_size("rad")
    pairs = [(i, i + by) for i in range(peers) if 0 <= i + by < peers]
    return lax.ppermute(array, "rad", pairs)


def wide(blocks):
    return jnp.concatenate(
        [blocks[core, chip] for chip in range(4) for core in range(2)], axis=1
    )


def apply(vector, matrix):
    return lax.dot_general(
        vector, matrix, (((1,), (1,)), ((), ())), preferred_element_type=F32
    )


def call(body, outs, *args, products=1):
    spec = pl.BlockSpec(memory_space=pltpu.VMEM)
    return pl.pallas_call(
        body,
        out_shape=[jax.ShapeDtypeStruct(shape, dtype) for shape, dtype in outs],
        in_specs=[spec] * len(args),
        out_specs=[spec] * len(outs),
        cost_estimate=pl.CostEstimate(
            flops=products * 2 * ROWS * 1024 * WIDTH,
            bytes_accessed=products * 1000000,
            transcendentals=0,
        ),
    )(*args)


BLOCK = ((ROWS, WIDTH), BF16)
TOTAL = ((ROWS, WIDTH), F32)


def middle_body(second, fourth, side, lift, middle):
    total = side[...].astype(F32) - apply(wide(second), lift[1, 0])
    middle[...] = (total - apply(wide(fourth), lift[1, 1])).astype(BF16)


def coarse_body(here, following, solve, total):
    total[...] = apply(wide(here), solve[0, 1]) + apply(wide(following), solve[0, 2])


def centre_body(middle, solve, coarse, centre):
    centre[...] = (apply(wide(middle), solve[0, 0]) - coarse[...]).astype(BF16)


def onward_body(fourth, middle, lifts, total):
    both = apply(wide(fourth), lifts[0]) + apply(wide(middle), lifts[1])
    total[...] = both.astype(BF16)


def reduced_body(second, middle, side, lift_one, lift_two, total):
    both = apply(wide(second), lift_one[0, 1]) + apply(wide(middle), lift_two[0, 1])
    total[...] = side[...].astype(F32) - both


def odd_body(second, fourth, here, following, solve, two, four):
    two[...] = apply(wide(second), solve[0, 0]) - apply(wide(here), solve[0, 1])
    four[...] = apply(wide(fourth), solve[1, 0]) - apply(wide(following), solve[1, 2])


def final_body(whole, solve, two, four, coarse, centre, total, before, solved, reduced):
    full = wide(whole)
    solved[0] = coarse[...]
    solved[1] = (two[...] - apply(full, solve[0, 2])).astype(BF16)
    solved[2] = centre[...]
    solved[3] = (four[...] - apply(full, solve[1, 1])).astype(BF16)
    reduced[0] = (total[...] - before[...].astype(F32)).astype(BF16)


def local(right_sides, coarse_solution, lift_one, solve_one, lift_two, solve_two):
    coarse_here = coarse_solution[0]
    coarse_next = passed_along(coarse_here, -1)
    lifts_next = passed_along(jnp.stack([lift_one[0, 0], lift_two[0, 0]]), -1)

    odd = over_chips(jnp.stack([right_sides[1], right_sides[3]]))
    second = over_cores(odd[:, 0])
    fourth = over_cores(odd[:, 1])
    coarse = over_chips(jnp.stack([coarse_here, coarse_next]))

    (middle,) = call(
        middle_body, [BLOCK], second, fourth, right_sides[2], lift_one, products=2
    )
    middle_part = over_chips(middle)
    here = over_cores(coarse[:, 0])
    following = over_cores(coarse[:, 1])
    (coarse_total,) = call(
        coarse_body, [TOTAL], here, following, solve_two, products=2
    )
    two, four = call(
        odd_body, [TOTAL, TOTAL], second, fourth, here, following, solve_one, products=4
    )
    middle_full = over_cores(middle_part)

    (centre,) = call(centre_body, [BLOCK], middle_full, solve_two, coarse_total)
    centre_part = over_chips(centre)
    (onward,) = call(
        onward_body, [BLOCK], fourth, middle_full, lifts_next, products=2
    )
    before = passed_along(onward, 1)
    (total,) = call(
        reduced_body,
        [TOTAL],
        second,
        middle_full,
        right_sides[0],
        lift_one,
        lift_two,
        products=2,
    )
    centre_full = over_cores(centre_part)
    solved, reduced = call(
        final_body,
        [((4, ROWS, WIDTH), BF16), ((1, ROWS, WIDTH), BF16)],
        centre_full,
        solve_one,
        two,
        four,
        coarse_here,
        centre,
        total,
        before,
        products=2,
    )
    return solved, reduced


def solution(mesh):
    return jax.shard_map(
        local,
        mesh=mesh,
        in_specs=(
            P("rad", None, "col"),
            P("rad", None, "col"),
            P("rad", None, "col", None),
            P("rad", None, "col", None),
            P("rad", None, "col", None),
            P("rad", None, "col", None),
        ),
        out_specs=(P("rad", None, "col"), P("rad", None, "col")),
        check_vma=False,
    )
```

```python
import jax
import jax.numpy as jnp
from jax import lax
from jax.experimental import pallas as pl
from jax.experimental.pallas import tpu as pltpu
from jax.sharding import PartitionSpec as P


ROWS = 384
HALF = 192
WIDTH = 128
BF16 = jnp.bfloat16
F32 = jnp.float32
VMEM = pl.BlockSpec(memory_space=pltpu.VMEM)
HBM = pl.BlockSpec(memory_space=pltpu.HBM)


def chips_of(peers):
    return [[i for i in range(peers) if i % 2 == core] for core in range(2)]


def over_chips(copies):
    groups = chips_of(lax.axis_size("col"))
    return lax.all_to_all(copies, "col", 0, 0, axis_index_groups=groups)


def from_partner(array):
    peers = lax.axis_size("col")
    return lax.ppermute(array, "col", [(i, i ^ 1) for i in range(peers)])


def passed_along(array, by):
    peers = lax.axis_size("rad")
    pairs = [(i, i + by) for i in range(peers) if 0 <= i + by < peers]
    return lax.ppermute(array, "rad", pairs)


def apply(vector, matrix):
    return lax.dot_general(
        vector, matrix, (((1,), (1,)), ((), ())), preferred_element_type=F32
    )


def core():
    return lax.rem(lax.axis_index("col"), 2)


def call(body, outs, *args, products=1, space=pltpu.VMEM):
    args = [pltpu.with_memory_space_constraint(arg, pltpu.VMEM) for arg in args]
    return pl.pallas_call(
        body,
        out_shape=[space(shape, dtype) for shape, dtype in outs],
        in_specs=[VMEM] * len(args),
        out_specs=[VMEM] * len(outs),
        compiler_params=pltpu.CompilerParams(vmem_limit_bytes=12 << 20),
        cost_estimate=pl.CostEstimate(
            flops=products * 2 * ROWS * 1024 * WIDTH,
            bytes_accessed=products * 1000000,
            transcendentals=0,
        ),
    )(*args)


PAIR = ((2, HALF, WIDTH), BF16)
TOTALS = ((2, HALF, WIDTH), F32)
COPIES = ((4, 2, HALF, WIDTH), BF16)


def from_eight(blocks, which):
    return jnp.concatenate([blocks[peer, which] for peer in range(8)], axis=1)


def from_four(blocks):
    return jnp.concatenate(
        [blocks[chip, side] for chip in range(4) for side in range(2)], axis=1
    )


def pack_body(sides, coarse, packed, held, arrived, sent):
    arrays = [sides.at[1], sides.at[3], coarse.at[0]]
    loads = [
        pltpu.make_async_copy(array, held.at[i], arrived.at[i])
        for i, array in enumerate(arrays)
    ]
    for load in loads:
        load.start()
    stores = []
    for i, load in enumerate(loads):
        load.wait()
        for peer in range(8):
            store = pltpu.make_async_copy(
                held.at[i, peer % 2], packed.at[peer, i], sent.at[i, peer]
            )
            store.start()
            stores.append(store)
    for store in stores:
        store.wait()


def pack(sides, coarse):
    return pl.pallas_call(
        pack_body,
        out_shape=pltpu.HBM((8, 3, HALF, WIDTH), BF16),
        in_specs=[HBM, HBM],
        out_specs=HBM,
        scratch_shapes=[
            pltpu.VMEM((3, 2, HALF, WIDTH), BF16),
            pltpu.SemaphoreType.DMA((3,)),
            pltpu.SemaphoreType.DMA((3, 8)),
        ],
        compiler_params=pltpu.CompilerParams(vmem_limit_bytes=4 << 20),
    )(
        pltpu.with_memory_space_constraint(sides, pltpu.HBM),
        pltpu.with_memory_space_constraint(coarse, pltpu.HBM),
    )


def spread(copies, own, partner):
    mine = core()
    for chip in range(4):
        copies[chip, mine] = own
        copies[chip, 1 - mine] = partner


def middle_body(odd, sides, sides_partner, lift, lift_partner, copies):
    second, fourth = from_eight(odd, 0), from_eight(odd, 1)
    results = []
    for side, matrices in ((sides, lift), (sides_partner, lift_partner)):
        total = side[2, core()].astype(F32) - apply(second, matrices[1, 0])
        results.append((total - apply(fourth, matrices[1, 1])).astype(BF16))
    spread(copies, *results)


def coarse_body(odd, following, solve, solve_partner, totals):
    here = from_eight(odd, 2)
    after = jnp.concatenate([following[peer] for peer in range(8)], axis=1)
    for i, matrices in enumerate((solve, solve_partner)):
        totals[i] = apply(here, matrices[0, 1]) + apply(after, matrices[0, 2])


def centre_body(middle, solve, solve_partner, coarse, copies):
    full = from_four(middle)
    results = [
        (apply(full, matrices[0, 0]) - coarse[i]).astype(BF16)
        for i, matrices in enumerate((solve, solve_partner))
    ]
    spread(copies, *results)


def onward_body(odd, middle, lifts, totals):
    fourth, full = from_eight(odd, 1), from_four(middle)
    for i in range(2):
        both = apply(fourth, lifts[2 * i]) + apply(full, lifts[2 * i + 1])
        totals[i] = both.astype(BF16)


def reduced_body(
    odd, middle, sides, sides_partner, one, one_partner, two, two_partner, totals
):
    second, full = from_eight(odd, 0), from_four(middle)
    for i, (side, first, last) in enumerate(
        ((sides, one, two), (sides_partner, one_partner, two_partner))
    ):
        both = apply(second, first[0, 1]) + apply(full, last[0, 1])
        totals[i] = side[0, core()].astype(F32) - both


def odd_body(odd, following, solve, solve_partner, two, four):
    second, fourth, here = (from_eight(odd, i) for i in range(3))
    after = jnp.concatenate([following[peer] for peer in range(8)], axis=1)
    for i, matrices in enumerate((solve, solve_partner)):
        two[i] = apply(second, matrices[0, 0]) - apply(here, matrices[0, 1])
        four[i] = apply(fourth, matrices[1, 0]) - apply(after, matrices[1, 2])


def final_body(
    centre, own, solve, solve_partner, two, four, totals, before, kept, given
):
    full = from_four(centre)
    for i, (matrices, out) in enumerate(((solve, kept), (solve_partner, given))):
        out[0] = (two[i] - apply(full, matrices[0, 2])).astype(BF16)
        out[1] = own[0, core() if i == 0 else 1 - core()]
        out[2] = (four[i] - apply(full, matrices[1, 1])).astype(BF16)
        out[3] = (totals[i] - before[i].astype(F32)).astype(BF16)


def place_body(coarse, kept, taken, solved, reduced):
    solved[0] = coarse[0]
    mine = core()
    for half, source in ((mine, kept), (1 - mine, taken)):
        for i in range(3):
            solved[i + 1, half] = source[i]
        reduced[0, half] = source[3]


def steps(right_sides, coarse_solution, lift_one, solve_one, lift_two, solve_two):
    sides = right_sides.reshape(4, 2, HALF, WIDTH)
    coarse = coarse_solution.reshape(1, 2, HALF, WIDTH)

    packed = pack(sides, coarse)
    odd = lax.all_to_all(packed, "col", 0, 0)
    sides_partner = from_partner(sides)
    one_partner = from_partner(lift_one)
    two_partner = from_partner(lift_two)
    solve_two_partner = from_partner(solve_two)
    solve_one_partner = from_partner(solve_one)
    lifts = jnp.stack(
        [lift_one[0, 0], lift_two[0, 0], one_partner[0, 0], two_partner[0, 0]]
    )
    lifts_next = passed_along(lifts, -1)
    following = passed_along(odd[:, 2], -1)

    (middle_copies,) = call(
        middle_body,
        [COPIES],
        odd,
        sides,
        sides_partner,
        lift_one,
        one_partner,
        products=2,
        space=pltpu.HBM,
    )
    middle = over_chips(middle_copies)
    (coarse_totals,) = call(
        coarse_body,
        [TOTALS],
        odd,
        following,
        solve_two,
        solve_two_partner,
        products=2,
    )
    two, four = call(
        odd_body,
        [TOTALS, TOTALS],
        odd,
        following,
        solve_one,
        solve_one_partner,
        products=4,
    )
    (centre_copies,) = call(
        centre_body,
        [COPIES],
        middle,
        solve_two,
        solve_two_partner,
        coarse_totals,
        space=pltpu.HBM,
    )
    centre = over_chips(centre_copies)
    (onward,) = call(onward_body, [PAIR], odd, middle, lifts_next, products=2)
    before = passed_along(onward, 1)
    (totals,) = call(
        reduced_body,
        [TOTALS],
        odd,
        middle,
        sides,
        sides_partner,
        lift_one,
        one_partner,
        lift_two,
        two_partner,
        products=2,
    )
    quads = ((4, HALF, WIDTH), BF16)
    kept, given = call(
        final_body,
        [quads, quads],
        centre,
        centre_copies,
        solve_one,
        solve_one_partner,
        two,
        four,
        totals,
        before,
        products=2,
    )
    solved, reduced = call(
        place_body,
        [((4, 2, HALF, WIDTH), BF16), ((1, 2, HALF, WIDTH), BF16)],
        coarse,
        kept,
        from_partner(given),
        space=jax.ShapeDtypeStruct,
    )
    return solved.reshape(4, ROWS, WIDTH), reduced.reshape(1, ROWS, WIDTH)


def solution(mesh):
    return jax.shard_map(
        steps,
        mesh=mesh,
        in_specs=(
            P("rad", None, "col"),
            P("rad", None, "col"),
            P("rad", None, "col", None),
            P("rad", None, "col", None),
            P("rad", None, "col", None),
            P("rad", None, "col", None),
        ),
        out_specs=(P("rad", None, "col"), P("rad", None, "col")),
        check_vma=False,
    )
```

```python
import jax
import jax.numpy as jnp
from jax import lax
from jax.experimental import pallas as pl
from jax.experimental.pallas import tpu as pltpu
from jax.sharding import PartitionSpec as P


ROWS = 384
HALF = 192
WIDTH = 128
BF16 = jnp.bfloat16
F32 = jnp.float32
VMEM = pl.BlockSpec(memory_space=pltpu.VMEM)
HBM = pl.BlockSpec(memory_space=pltpu.HBM)


def chips_of(peers):
    return [[i for i in range(peers) if i % 2 == core] for core in range(2)]


def over_chips(copies):
    groups = chips_of(lax.axis_size("col"))
    return lax.all_to_all(copies, "col", 0, 0, axis_index_groups=groups)


def from_partner(array):
    peers = lax.axis_size("col")
    return lax.ppermute(array, "col", [(i, i ^ 1) for i in range(peers)])


def passed_along(array, by):
    peers = lax.axis_size("rad")
    pairs = [(i, i + by) for i in range(peers) if 0 <= i + by < peers]
    return lax.ppermute(array, "rad", pairs)


def apply(vector, matrix):
    return lax.dot_general(
        vector, matrix, (((1,), (1,)), ((), ())), preferred_element_type=F32
    )


def core():
    return lax.rem(lax.axis_index("col"), 2)


class Part:
    def __init__(self, array, index=()):
        self.array, self.index = array, index
        self.shape = array.shape[len(index) :]

    def load(self, source, held, sem):
        index = tuple(i() if callable(i) else i for i in self.index)
        self.held, self.ready = held, False
        self.copy = pltpu.make_async_copy(
            source.at[index] if index else source, held, sem
        )
        self.copy.start()

    def __getitem__(self, index):
        if not self.ready:
            self.copy.wait()
            self.ready = True
        return self.held[index]


def call(body, outs, whole, parts, products=1, space=pltpu.HBM):
    count, pieces = len(whole), len(parts)

    def kernel(*refs):
        sources = refs[count : count + pieces]
        results = refs[count + pieces : count + pieces + len(outs)]
        held, sems = refs[count + pieces + len(outs) : -1], refs[-1]
        for i, part in enumerate(parts):
            part.load(sources[i], held[i], sems.at[i])
        body(*refs[:count], *parts, *results)

    return pl.pallas_call(
        kernel,
        out_shape=[space(shape, dtype) for shape, dtype in outs],
        in_specs=[VMEM] * count + [HBM] * pieces,
        out_specs=[VMEM] * len(outs),
        scratch_shapes=[pltpu.VMEM(part.shape, part.array.dtype) for part in parts]
        + [pltpu.SemaphoreType.DMA((pieces,))],
        compiler_params=pltpu.CompilerParams(vmem_limit_bytes=12 << 20),
        cost_estimate=pl.CostEstimate(
            flops=products * 2 * ROWS * 1024 * WIDTH,
            bytes_accessed=products * 1000000,
            transcendentals=0,
        ),
    )(
        *[pltpu.with_memory_space_constraint(array, pltpu.VMEM) for array in whole],
        *[pltpu.with_memory_space_constraint(p.array, pltpu.HBM) for p in parts],
    )


PAIR = ((2, HALF, WIDTH), BF16)
TOTALS = ((2, HALF, WIDTH), F32)
COPIES = ((4, 2, HALF, WIDTH), BF16)


def from_eight(blocks, which):
    return jnp.concatenate([blocks[peer, which] for peer in range(8)], axis=1)


def from_four(blocks):
    return jnp.concatenate(
        [blocks[chip, side] for chip in range(4) for side in range(2)], axis=1
    )


def pack_body(sides, coarse, packed, held, arrived, sent):
    arrays = [sides.at[1], sides.at[3], coarse.at[0]]
    loads = [
        pltpu.make_async_copy(array, held.at[i], arrived.at[i])
        for i, array in enumerate(arrays)
    ]
    for load in loads:
        load.start()
    stores = []
    for i, load in enumerate(loads):
        load.wait()
        for peer in range(8):
            store = pltpu.make_async_copy(
                held.at[i, peer % 2], packed.at[peer, i], sent.at[i, peer]
            )
            store.start()
            stores.append(store)
    for store in stores:
        store.wait()


def pack(sides, coarse):
    return pl.pallas_call(
        pack_body,
        out_shape=pltpu.HBM((8, 3, HALF, WIDTH), BF16),
        in_specs=[HBM, HBM],
        out_specs=HBM,
        scratch_shapes=[
            pltpu.VMEM((3, 2, HALF, WIDTH), BF16),
            pltpu.SemaphoreType.DMA((3,)),
            pltpu.SemaphoreType.DMA((3, 8)),
        ],
        compiler_params=pltpu.CompilerParams(vmem_limit_bytes=4 << 20),
    )(
        pltpu.with_memory_space_constraint(sides, pltpu.HBM),
        pltpu.with_memory_space_constraint(coarse, pltpu.HBM),
    )


def spread(copies, own, partner):
    mine = core()
    for chip in range(4):
        copies[chip, mine] = own
        copies[chip, 1 - mine] = partner


def from_following(following):
    return jnp.concatenate([following[peer] for peer in range(8)], axis=1)


def middle_body(odd, one, one_partner, side, side_partner, copies):
    second, fourth = from_eight(odd, 0), from_eight(odd, 1)
    results = []
    for begun, matrices in ((side, one), (side_partner, one_partner)):
        both = apply(second, matrices[0]) + apply(fourth, matrices[1])
        results.append((begun[...].astype(F32) - both).astype(BF16))
    spread(copies, *results)


def coarse_body(odd, solve, solve_partner, following, totals):
    here = from_eight(odd, 2)
    for i, matrices in enumerate((solve, solve_partner)):
        totals[i] = apply(here, matrices[1])
    after = from_following(following)
    for i, matrices in enumerate((solve, solve_partner)):
        totals[i] += apply(after, matrices[2])


def centre_body(middle, solve, solve_partner, coarse, copies):
    full = from_four(middle)
    results = [
        (apply(full, matrix[...]) - coarse[i]).astype(BF16)
        for i, matrix in enumerate((solve, solve_partner))
    ]
    spread(copies, *results)


def onward_body(odd, middle, lifts, lifts_partner, totals):
    fourth, full = from_eight(odd, 1), from_four(middle)
    for i, matrices in enumerate((lifts, lifts_partner)):
        both = apply(fourth, matrices[0]) + apply(full, matrices[1])
        totals[i] = both.astype(BF16)


def reduced_body(
    odd, middle, one, one_partner, two, two_partner, side, side_partner, totals
):
    second, full = from_eight(odd, 0), from_four(middle)
    for i, (begun, first, last) in enumerate(
        ((side, one, two), (side_partner, one_partner, two_partner))
    ):
        both = apply(second, first[...]) + apply(full, last[...])
        totals[i] = begun[...].astype(F32) - both


def odd_body(odd, one, one_partner, three, three_partner, following, totals):
    second, fourth, here = (from_eight(odd, i) for i in range(3))
    for i, matrices in enumerate((one, one_partner)):
        totals[0, i] = apply(second, matrices[0]) - apply(here, matrices[1])
    after = from_following(following)
    for i, matrices in enumerate((three, three_partner)):
        totals[1, i] = apply(fourth, matrices[0]) - apply(after, matrices[2])


def final_body(
    centre, one, one_partner, three, three_partner, odd, own, totals, before,
    kept, given,
):
    full = from_four(centre)
    mine = core()
    for i, (first, last, out) in enumerate(
        ((one, three, kept), (one_partner, three_partner, given))
    ):
        out[0] = (odd[0, i] - apply(full, first[...])).astype(BF16)
        out[1] = own[mine if i == 0 else 1 - mine]
        out[2] = (odd[1, i] - apply(full, last[...])).astype(BF16)
        out[3] = (totals[i] - before[i].astype(F32)).astype(BF16)


def place_body(taken, coarse, kept, solved, reduced):
    mine = core()
    solved[0] = coarse[...]
    for i in range(3):
        solved[i + 1, mine] = kept[i]
        solved[i + 1, 1 - mine] = taken[1 - mine, i]
    reduced[0, mine] = kept[3]
    reduced[0, 1 - mine] = taken[1 - mine, 3]


def steps(right_sides, coarse_solution, lift_one, solve_one, lift_two, solve_two):
    sides = right_sides.reshape(4, 2, HALF, WIDTH)
    coarse = coarse_solution.reshape(1, 2, HALF, WIDTH)
    packed = pack(sides, coarse)
    odd = lax.all_to_all(packed, "col", 0, 0)
    lifts = jnp.stack([lift_one[0, 0], lift_two[0, 0]])
    lifts_next = passed_along(lifts, -1)
    one_partner = from_partner(lift_one)
    sides_partner = from_partner(sides)
    solve_two_partner = from_partner(solve_two)
    solve_one_partner = from_partner(solve_one)
    two_partner = from_partner(lift_two)
    following = passed_along(odd[:, 2], -1)
    lifts_partner = from_partner(lifts_next)

    (middle_copies,) = call(
        middle_body,
        [COPIES],
        [odd],
        [
            Part(lift_one, (1,)),
            Part(one_partner, (1,)),
            Part(sides, (2, core)),
            Part(sides_partner, (2, core)),
        ],
        products=2,
    )
    middle = over_chips(middle_copies)
    (coarse_totals,) = call(
        coarse_body,
        [TOTALS],
        [odd],
        [Part(solve_two, (0,)), Part(solve_two_partner, (0,)), Part(following)],
        products=2,
    )
    (odd_totals,) = call(
        odd_body,
        [((2, 2, HALF, WIDTH), F32)],
        [odd],
        [
            Part(solve_one, (0,)),
            Part(solve_one_partner, (0,)),
            Part(solve_one, (1,)),
            Part(solve_one_partner, (1,)),
            Part(following),
        ],
        products=4,
    )
    (centre_copies,) = call(
        centre_body,
        [COPIES],
        [middle],
        [
            Part(solve_two, (0, 0)),
            Part(solve_two_partner, (0, 0)),
            Part(coarse_totals),
        ],
    )
    centre = over_chips(centre_copies)
    (onward,) = call(
        onward_body,
        [PAIR],
        [odd, middle],
        [Part(lifts_next), Part(lifts_partner)],
        products=2,
    )
    before = passed_along(onward, 1)
    (totals,) = call(
        reduced_body,
        [TOTALS],
        [odd, middle],
        [
            Part(lift_one, (0, 1)),
            Part(one_partner, (0, 1)),
            Part(lift_two, (0, 1)),
            Part(two_partner, (0, 1)),
            Part(sides, (0, core)),
            Part(sides_partner, (0, core)),
        ],
        products=2,
    )
    quads = ((4, HALF, WIDTH), BF16)
    kept, given = call(
        final_body,
        [quads, quads],
        [centre],
        [
            Part(solve_one, (0, 2)),
            Part(solve_one_partner, (0, 2)),
            Part(solve_one, (1, 1)),
            Part(solve_one_partner, (1, 1)),
            Part(odd_totals),
            Part(centre_copies, (0,)),
            Part(totals),
            Part(before),
        ],
        products=2,
    )
    cores = [[i, i + 1] for i in range(0, lax.axis_size("col"), 2)]
    taken = lax.all_gather(given, "col", axis=0, axis_index_groups=cores)
    solved, reduced = call(
        place_body,
        [((4, 2, HALF, WIDTH), BF16), ((1, 2, HALF, WIDTH), BF16)],
        [taken],
        [Part(coarse, (0,)), Part(kept)],
    )
    return solved.reshape(4, ROWS, WIDTH), reduced.reshape(1, ROWS, WIDTH)


def solution(mesh):
    return jax.shard_map(
        steps,
        mesh=mesh,
        in_specs=(
            P("rad", None, "col"),
            P("rad", None, "col"),
            P("rad", None, "col", None),
            P("rad", None, "col", None),
            P("rad", None, "col", None),
            P("rad", None, "col", None),
        ),
        out_specs=(P("rad", None, "col"), P("rad", None, "col")),
        check_vma=False,
    )
```

```python
import jax
import jax.numpy as jnp
from jax import lax
from jax.experimental import pallas as pl
from jax.experimental.pallas import tpu as pltpu
from jax.sharding import PartitionSpec as P


ANY = pl.BlockSpec(memory_space=pl.ANY)
ROWS = 384
HALF = 192
WIDTH = 128
BF16 = jnp.bfloat16
F32 = jnp.float32
VMEM = pl.BlockSpec(memory_space=pltpu.VMEM)
HBM = pl.BlockSpec(memory_space=pltpu.HBM)


def chips_of(peers):
    return [[i for i in range(peers) if i % 2 == core] for core in range(2)]


def over_chips(copies):
    groups = chips_of(lax.axis_size("col"))
    return lax.all_to_all(copies, "col", 0, 0, axis_index_groups=groups)


def from_partner(array):
    peers = lax.axis_size("col")
    return lax.ppermute(array, "col", [(i, i ^ 1) for i in range(peers)])


def passed_along(array, by):
    peers = lax.axis_size("rad")
    pairs = [(i, i + by) for i in range(peers) if 0 <= i + by < peers]
    return lax.ppermute(array, "rad", pairs)


def apply(vector, matrix):
    return lax.dot_general(
        vector, matrix, (((1,), (1,)), ((), ())), preferred_element_type=F32
    )


def core():
    return lax.rem(lax.axis_index("col"), 2)


class Pieces:
    def __init__(self, sems):
        self.sems, self.copies = sems, []

    def load(self, source, held):
        sem = self.sems.at[len(self.copies)]
        copy = pltpu.make_async_copy(source, held, sem)
        copy.start()
        self.copies.append(copy)
        return copy

    def both(self, own, partner, held):
        return (
            self.load(own, held.at[pl.ds(0, WIDTH)]),
            self.load(partner, held.at[pl.ds(WIDTH, WIDTH)]),
        )

    def wait(self):
        for copy in self.copies:
            copy.wait()


def call(body, outs, whole, parts=(), scratch=(), copies=0, products=1, free=()):
    return pl.pallas_call(
        body,
        out_shape=[space(shape, dtype) for space, shape, dtype in outs],
        in_specs=[VMEM] * len(whole)
        + [HBM] * len(parts)
        + [ANY] * len(free),
        out_specs=[VMEM] * len(outs),
        scratch_shapes=[pltpu.VMEM(*one) for one in scratch]
        + [pltpu.SemaphoreType.DMA((max(copies, 1),))],
        compiler_params=pltpu.CompilerParams(vmem_limit_bytes=12 << 20),
        cost_estimate=pl.CostEstimate(
            flops=products * 2 * ROWS * 1024 * WIDTH,
            bytes_accessed=products * 1000000,
            transcendentals=0,
        ),
    )(
        *[pltpu.with_memory_space_constraint(x, pltpu.VMEM) for x in whole],
        *[pltpu.with_memory_space_constraint(x, pltpu.HBM) for x in parts],
        *free,
    )


IN_VMEM, IN_HBM = pltpu.VMEM, pltpu.HBM
PAIR = (2, HALF, WIDTH)
COPIES = (4, 2, HALF, WIDTH)
MERGED = (2 * WIDTH, 1024)


def from_eight(blocks, which):
    return jnp.concatenate([blocks[peer, which] for peer in range(8)], axis=1)


def from_four(blocks):
    return jnp.concatenate(
        [blocks[chip, side] for chip in range(4) for side in range(2)], axis=1
    )


def pack_body(sides, coarse, packed, held, arrived, sent):
    arrays = [sides.at[1], sides.at[3], coarse.at[0]]
    loads = [
        pltpu.make_async_copy(array, held.at[i], arrived.at[i])
        for i, array in enumerate(arrays)
    ]
    for load in loads:
        load.start()
    stores = []
    for i, load in enumerate(loads):
        load.wait()
        for peer in range(8):
            store = pltpu.make_async_copy(
                held.at[i, peer % 2], packed.at[peer, i], sent.at[i, peer]
            )
            store.start()
            stores.append(store)
    for store in stores:
        store.wait()


def pack(sides, coarse):
    return pl.pallas_call(
        pack_body,
        out_shape=pltpu.HBM((8, 3, HALF, WIDTH), BF16),
        in_specs=[HBM, HBM],
        out_specs=HBM,
        scratch_shapes=[
            pltpu.VMEM((3, 2, HALF, WIDTH), BF16),
            pltpu.SemaphoreType.DMA((3,)),
            pltpu.SemaphoreType.DMA((3, 8)),
        ],
        compiler_params=pltpu.CompilerParams(vmem_limit_bytes=4 << 20),
    )(
        pltpu.with_memory_space_constraint(sides, pltpu.HBM),
        pltpu.with_memory_space_constraint(coarse, pltpu.HBM),
    )


def from_following(following):
    return jnp.concatenate([following[peer] for peer in range(8)], axis=1)


def own_and_partner(total):
    return total[:, :WIDTH], total[:, WIDTH:]


def spread(copies, results):
    mine = core()
    for chip in range(4):
        copies[chip, mine] = results[0]
        copies[chip, 1 - mine] = results[1]


def lifts_body(one, two, out, sems):
    pieces = Pieces(sems)
    pieces.load(one.at[0, 0], out.at[0])
    pieces.load(two.at[0, 0], out.at[1])
    pieces.wait()


def prepare_body(one, one_partner, sides, sides_partner, matrices, begun, sems):
    pieces, mine = Pieces(sems), core()
    for i in range(2):
        pieces.both(one.at[1, i], one_partner.at[1, i], matrices.at[i])
    pieces.load(sides.at[2, mine], begun.at[0])
    pieces.load(sides_partner.at[2, mine], begun.at[1])
    pieces.wait()


def middle_body(odd, matrices, begun, copies, sems):
    total = apply(from_eight(odd, 0), matrices[0])
    total += apply(from_eight(odd, 1), matrices[1])
    spread(
        copies,
        [
            (begun[i].astype(F32) - part).astype(BF16)
            for i, part in enumerate(own_and_partner(total))
        ],
    )


def early_body(
    odd, one, one_partner, solve, solve_partner, last, last_partner,
    inverse, coarse, ends, lifted, held, sems,
):
    pieces = Pieces(sems)
    waits = [
        pieces.both(own.at[index], partner.at[index], held.at[i])
        for i, (own, partner, index) in enumerate(
            (
                (last, last_partner, (0, 1)),
                (solve, solve_partner, (0, 0)),
                (solve, solve_partner, (0, 1)),
                (solve, solve_partner, (1, 0)),
                (one, one_partner, (0, 1)),
            )
        )
    ]
    waits.append(pieces.both(last.at[0, 0], last_partner.at[0, 0], inverse))

    def product(vector, i):
        for copy in waits[i]:
            copy.wait()
        return apply(vector, held[i])

    second, fourth, here = (from_eight(odd, i) for i in range(3))
    coarse[...] = product(here, 0)
    ends[0] = product(second, 1) - product(here, 2)
    ends[1] = product(fourth, 3)
    lifted[...] = product(second, 4)
    for copy in waits[5]:
        copy.wait()


def late_body(
    odd, coarse, solve, solve_partner, last, last_partner, lifts, lifts_partner,
    following, totals, end, onward, held, arrived, sems,
):
    pieces = Pieces(sems)
    waits = [
        pieces.both(own.at[index], partner.at[index], held.at[i])
        for i, (own, partner, index) in enumerate(
            (
                (lifts, lifts_partner, (0,)),
                (last, last_partner, (0, 2)),
                (solve, solve_partner, (1, 2)),
            )
        )
    ]
    arrival = pieces.load(following, arrived)

    def product(vector, i):
        for copy in waits[i]:
            copy.wait()
        return apply(vector, held[i])

    onward[...] = product(from_eight(odd, 1), 0)
    arrival.wait()
    after = from_following(arrived)
    totals[...] = coarse[...] + product(after, 1)
    end[...] = product(after, 2)


def centre_body(middle, inverse, coarse, copies, sems):
    total = apply(from_four(middle), inverse[...]) - coarse[...]
    spread(copies, [part.astype(BF16) for part in own_and_partner(total)])


def onward_body(middle, begun, lifts, lifts_partner, totals, held, sems):
    pieces = Pieces(sems)
    pieces.both(lifts.at[1], lifts_partner.at[1], held)
    full = from_four(middle)
    pieces.wait()
    total = begun[...] + apply(full, held[...])
    for i, part in enumerate(own_and_partner(total)):
        totals[i] = part.astype(BF16)


def reduced_body(
    middle, two, solve, solve_partner, sides, sides_partner, lifted, ends, end, coarse,
    two_partner, total, matrices, begun, kept, held, sides_held, late, sems,
):
    pieces, mine = Pieces(sems), core()
    pieces.both(two.at[0, 1], two_partner.at[0, 1], held)
    pieces.load(sides.at[0, mine], sides_held.at[0])
    pieces.load(sides_partner.at[0, mine], sides_held.at[1])
    pieces.load(lifted, late.at[0])
    pieces.load(end, late.at[1])
    pieces.load(ends, begun)
    pieces.both(solve.at[0, 2], solve_partner.at[0, 2], matrices.at[0])
    pieces.both(solve.at[1, 1], solve_partner.at[1, 1], matrices.at[1])
    pieces.load(coarse.at[0], kept)
    full = from_four(middle)
    pieces.wait()
    both = late[0] + apply(full, held[...])
    for i, part in enumerate(own_and_partner(both)):
        total[i] = sides_held[i].astype(F32) - part
    begun[1] -= late[1]


def final_body(centre, matrices, begun, total, before, kept, given, sems):
    full = from_four(centre)
    chip, mine = lax.div(lax.axis_index("col"), 2), core()
    first = begun[0] - apply(full, matrices[0])
    last = begun[1] - apply(full, matrices[1])
    for i, out in enumerate((kept, given)):
        out[0] = own_and_partner(first)[i].astype(BF16)
        out[1] = centre[chip, mine if i == 0 else 1 - mine]
        out[2] = own_and_partner(last)[i].astype(BF16)
        out[3] = (total[i] - before[i].astype(F32)).astype(BF16)


def place_body(taken, coarse, kept, solved, reduced, sems):
    mine = core()
    solved[0] = coarse[...]
    for i in range(3):
        solved[i + 1, mine] = kept[i]
        solved[i + 1, 1 - mine] = taken[1 - mine, i]
    reduced[0, mine] = kept[3]
    reduced[0, 1 - mine] = taken[1 - mine, 3]


def steps(right_sides, coarse_solution, lift_one, solve_one, lift_two, solve_two):
    sides = right_sides.reshape(4, 2, HALF, WIDTH)
    coarse = coarse_solution.reshape(1, 2, HALF, WIDTH)
    packed = pack(sides, coarse)
    odd = lax.all_to_all(packed, "col", 0, 0)
    (lifts,) = call(
        lifts_body,
        [(IN_HBM, (2, WIDTH, 1024), BF16)],
        [],
        [lift_one, lift_two],
        copies=2,
    )
    lifts_next = passed_along(lifts, -1)
    one_partner = from_partner(lift_one)
    sides_partner = from_partner(sides)
    solve_two_partner = from_partner(solve_two)
    solve_one_partner = from_partner(solve_one)
    two_partner = from_partner(lift_two)
    following = passed_along(odd[:, 2], -1)
    lifts_partner = from_partner(lifts_next)

    lift_matrices, begun = call(
        prepare_body,
        [(IN_VMEM, (2, *MERGED), BF16), (IN_VMEM, PAIR, BF16)],
        [],
        [lift_one, one_partner, sides],
        copies=6,
        free=[sides_partner],
    )
    (middle_copies,) = call(
        middle_body,
        [(IN_HBM, COPIES, BF16)],
        [odd, lift_matrices, begun],
        products=2,
    )
    middle = over_chips(middle_copies)
    flat = (HALF, 2 * WIDTH)
    inverse, coarse_begun, ends, lifted = call(
        early_body,
        [
            (IN_VMEM, MERGED, BF16),
            (IN_VMEM, flat, F32),
            (IN_HBM, (2, *flat), F32),
            (IN_HBM, flat, F32),
        ],
        [odd],
        [
            lift_one,
            one_partner,
            solve_one,
            solve_one_partner,
            solve_two,
            solve_two_partner,
        ],
        [((5, *MERGED), BF16)],
        copies=12,
        products=5,
    )
    coarse_total, end, onward_begun = call(
        late_body,
        [(IN_VMEM, flat, F32), (IN_HBM, flat, F32), (IN_VMEM, flat, F32)],
        [odd, coarse_begun],
        [
            solve_one,
            solve_one_partner,
            solve_two,
            solve_two_partner,
            lifts_next,
        ],
        [((3, *MERGED), BF16), ((8, HALF, WIDTH), BF16)],
        free=[lifts_partner, following],
        copies=7,
        products=3,
    )
    (centre_copies,) = call(
        centre_body, [(IN_HBM, COPIES, BF16)], [middle, inverse, coarse_total]
    )
    centre = over_chips(centre_copies)
    (onward,) = call(
        onward_body,
        [(IN_VMEM, PAIR, BF16)],
        [middle, onward_begun],
        [lifts_next],
        [(MERGED, BF16)],
        free=[lifts_partner],
        copies=2,
    )
    before = passed_along(onward, 1)
    total, solve_matrices, ends_begun, coarse_kept = call(
        reduced_body,
        [
            (IN_VMEM, PAIR, F32),
            (IN_VMEM, (2, *MERGED), BF16),
            (IN_VMEM, (2, *flat), F32),
            (IN_VMEM, PAIR, BF16),
        ],
        [middle],
        [
            lift_two,
            solve_one,
            solve_one_partner,
            sides,
            sides_partner,
            lifted,
            ends,
            end,
            coarse,
        ],
        [(MERGED, BF16), (PAIR, BF16), ((2, *flat), F32)],
        copies=12,
        products=2,
        free=[two_partner],
    )
    kept, given = call(
        final_body,
        [(IN_VMEM, (4, HALF, WIDTH), BF16)] * 2,
        [centre, solve_matrices, ends_begun, total, before],
        products=2,
    )
    cores = [[i, i + 1] for i in range(0, lax.axis_size("col"), 2)]
    taken = lax.all_gather(given, "col", axis=0, axis_index_groups=cores)
    solved, reduced = call(
        place_body,
        [
            (IN_HBM, (4, 2, HALF, WIDTH), BF16),
            (IN_HBM, (1, 2, HALF, WIDTH), BF16),
        ],
        [taken, coarse_kept, kept],
    )
    return solved.reshape(4, ROWS, WIDTH), reduced.reshape(1, ROWS, WIDTH)


def solution(mesh):
    return jax.shard_map(
        steps,
        mesh=mesh,
        in_specs=(
            P("rad", None, "col"),
            P("rad", None, "col"),
            P("rad", None, "col", None),
            P("rad", None, "col", None),
            P("rad", None, "col", None),
            P("rad", None, "col", None),
        ),
        out_specs=(P("rad", None, "col"), P("rad", None, "col")),
        check_vma=False,
    )
```

```python
import jax
import jax.numpy as jnp
from jax import lax
from jax.experimental import pallas as pl
from jax.experimental.pallas import tpu as pltpu
from jax.sharding import PartitionSpec as P


ANY = pl.BlockSpec(memory_space=pl.ANY)
ROWS = 384
HALF = 192
WIDTH = 128
BF16 = jnp.bfloat16
F32 = jnp.float32
VMEM = pl.BlockSpec(memory_space=pltpu.VMEM)
HBM = pl.BlockSpec(memory_space=pltpu.HBM)


def chips_of(peers):
    return [[i for i in range(peers) if i % 2 == core] for core in range(2)]


def over_chips(copies):
    groups = chips_of(lax.axis_size("col"))
    return lax.all_to_all(copies, "col", 0, 0, axis_index_groups=groups)


def from_partner(array):
    peers = lax.axis_size("col")
    return lax.ppermute(array, "col", [(i, i ^ 1) for i in range(peers)])


def passed_along(array, by):
    peers = lax.axis_size("rad")
    pairs = [(i, i + by) for i in range(peers) if 0 <= i + by < peers]
    return lax.ppermute(array, "rad", pairs)


def apply(vector, matrix):
    return lax.dot_general(
        vector, matrix, (((1,), (1,)), ((), ())), preferred_element_type=F32
    )


def core():
    return lax.rem(lax.axis_index("col"), 2)


class Pieces:
    def __init__(self, sems):
        self.sems, self.copies = sems, []

    def load(self, source, held):
        sem = self.sems.at[len(self.copies)]
        copy = pltpu.make_async_copy(source, held, sem)
        copy.start()
        self.copies.append(copy)
        return copy

    def both(self, own, partner, held):
        return (
            self.load(own, held.at[pl.ds(0, WIDTH)]),
            self.load(partner, held.at[pl.ds(WIDTH, WIDTH)]),
        )

    def wait(self):
        for copy in self.copies:
            copy.wait()


def call(body, outs, whole, parts=(), scratch=(), copies=0, products=1, free=()):
    return pl.pallas_call(
        body,
        out_shape=[space(shape, dtype) for space, shape, dtype in outs],
        in_specs=[VMEM] * len(whole)
        + [HBM] * len(parts)
        + [ANY] * len(free),
        out_specs=[VMEM] * len(outs),
        scratch_shapes=[pltpu.VMEM(*one) for one in scratch]
        + [pltpu.SemaphoreType.DMA((max(copies, 1),))],
        compiler_params=pltpu.CompilerParams(vmem_limit_bytes=12 << 20),
        cost_estimate=pl.CostEstimate(
            flops=products * 2 * ROWS * 1024 * WIDTH,
            bytes_accessed=products * 1000000,
            transcendentals=0,
        ),
    )(
        *[pltpu.with_memory_space_constraint(x, pltpu.VMEM) for x in whole],
        *[pltpu.with_memory_space_constraint(x, pltpu.HBM) for x in parts],
        *free,
    )


IN_VMEM, IN_HBM = pltpu.VMEM, pltpu.HBM
PAIR = (2, HALF, WIDTH)
COPIES = (4, 2, HALF, WIDTH)
MERGED = (2 * WIDTH, 1024)
STRIPS, STRIP = 4, 48


def from_eight(blocks, which):
    return jnp.concatenate([blocks[peer, which] for peer in range(8)], axis=1)


def from_four(blocks):
    return jnp.concatenate(
        [blocks[chip, side] for chip in range(4) for side in range(2)], axis=1
    )


def pack_body(sides, coarse, packed, held, arrived, sent):
    arrays = [sides.at[1], sides.at[3], coarse.at[0]]
    loads = [
        pltpu.make_async_copy(array, held.at[i], arrived.at[i])
        for i, array in enumerate(arrays)
    ]
    for load in loads:
        load.start()
    stores = []
    for i, load in enumerate(loads):
        load.wait()
        for peer in range(8):
            store = pltpu.make_async_copy(
                held.at[i, peer % 2], packed.at[peer, i], sent.at[i, peer]
            )
            store.start()
            stores.append(store)
    for store in stores:
        store.wait()


def pack(sides, coarse):
    return pl.pallas_call(
        pack_body,
        out_shape=pltpu.HBM((8, 3, HALF, WIDTH), BF16),
        in_specs=[HBM, HBM],
        out_specs=HBM,
        scratch_shapes=[
            pltpu.VMEM((3, 2, HALF, WIDTH), BF16),
            pltpu.SemaphoreType.DMA((3,)),
            pltpu.SemaphoreType.DMA((3, 8)),
        ],
        compiler_params=pltpu.CompilerParams(vmem_limit_bytes=4 << 20),
    )(
        pltpu.with_memory_space_constraint(sides, pltpu.HBM),
        pltpu.with_memory_space_constraint(coarse, pltpu.HBM),
    )


def from_following(following):
    return jnp.concatenate([following[peer] for peer in range(8)], axis=1)


def own_and_partner(total):
    return total[:, :WIDTH], total[:, WIDTH:]


def spread(copies, results):
    mine = core()
    for chip in range(4):
        copies[chip, mine] = results[0]
        copies[chip, 1 - mine] = results[1]


def bundle_body(
    one, two, solve_one, solve_two, sides, bundle, lifts, held, lifts_held, arrived, sent
):
    other = 1 - core()
    incoming, outgoing = Pieces(arrived), Pieces(sent)
    groups = (
        (one.at[0, 0], lifts_held.at[0], lifts.at[0]),
        (two.at[0, 0], lifts_held.at[1], lifts.at[1]),
        (one.at[1], held.at[pl.ds(0, 2)], bundle.at[pl.ds(0, 2)]),
        (one.at[0, 1], held.at[2], bundle.at[2]),
        (two.at[0, 1], held.at[3], bundle.at[3]),
        (solve_two.at[0], held.at[pl.ds(4, 3)], bundle.at[pl.ds(4, 3)]),
        (solve_one.at[0], held.at[pl.ds(7, 3)], bundle.at[pl.ds(7, 3)]),
        (solve_one.at[1], held.at[pl.ds(10, 3)], bundle.at[pl.ds(10, 3)]),
    )
    loads = [incoming.load(source, place) for source, place, _ in groups]
    rows = []
    for j in range(2 * STRIPS):
        strip = sides.at[2 * (j // STRIPS), other, pl.ds(STRIP * (j % STRIPS), STRIP)]
        rows.append(incoming.load(strip, strip_of(held, j)))
    for load, (_, place, target) in zip(loads, groups):
        load.wait()
        outgoing.load(place, target)
    for row in rows:
        row.wait()
    outgoing.load(held.at[13, pl.ds(0, STRIP)], bundle.at[13, pl.ds(0, STRIP)])
    outgoing.wait()


def strip_of(bundle, j):
    return bundle.at[13, pl.ds(0, STRIP), pl.ds(WIDTH * j, WIDTH)]


def bundled(*arrays):
    return pl.pallas_call(
        bundle_body,
        out_shape=[
            pltpu.HBM((14, WIDTH, 1024), BF16),
            pltpu.HBM((2, WIDTH, 1024), BF16),
        ],
        in_specs=[HBM] * len(arrays),
        out_specs=[HBM] * 2,
        scratch_shapes=[
            pltpu.VMEM((14, WIDTH, 1024), BF16),
            pltpu.VMEM((2, WIDTH, 1024), BF16),
            pltpu.SemaphoreType.DMA((8 + 2 * STRIPS,)),
            pltpu.SemaphoreType.DMA((9,)),
        ],
        compiler_params=pltpu.CompilerParams(vmem_limit_bytes=12 << 20),
        cost_estimate=pl.CostEstimate(
            flops=0, bytes_accessed=9000000, transcendentals=0
        ),
    )(*[pltpu.with_memory_space_constraint(x, pltpu.HBM) for x in arrays])


def load_sides(pieces, which, sides, bundle, held):
    pieces.load(sides.at[2 * which, core()], held.at[0])
    for j in range(STRIPS):
        place = held.at[1, pl.ds(STRIP * j, STRIP)]
        pieces.load(strip_of(bundle, STRIPS * which + j), place)


def prepare_body(one, bundle, sides, matrices, begun, sems):
    pieces = Pieces(sems)
    for i in range(2):
        pieces.both(one.at[1, i], bundle.at[i], matrices.at[i])
    load_sides(pieces, 1, sides, bundle, begun)
    pieces.wait()


def middle_body(odd, matrices, begun, copies, sems):
    total = apply(from_eight(odd, 0), matrices[0])
    total += apply(from_eight(odd, 1), matrices[1])
    spread(
        copies,
        [
            (begun[i].astype(F32) - part).astype(BF16)
            for i, part in enumerate(own_and_partner(total))
        ],
    )


def early_body(
    odd, one, solve, last, bundle, lifts, lifts_partner,
    inverses, coarse, early, onward, held, sems,
):
    pieces = Pieces(sems)
    waits = [
        pieces.both(own, partner, held.at[i])
        for i, (own, partner) in enumerate(
            (
                (last.at[0, 1], bundle.at[5]),
                (solve.at[0, 0], bundle.at[7]),
                (solve.at[0, 1], bundle.at[8]),
                (solve.at[1, 0], bundle.at[10]),
                (one.at[0, 1], bundle.at[2]),
                (lifts.at[0], lifts_partner.at[0]),
            )
        )
    ]
    rest = pieces.both(last.at[0, 0], bundle.at[4], inverses.at[0])
    rest += pieces.both(last.at[0, 2], bundle.at[6], inverses.at[1])

    def product(vector, i):
        for copy in waits[i]:
            copy.wait()
        return apply(vector, held[i])

    second, fourth, here = (from_eight(odd, i) for i in range(3))
    coarse[...] = product(here, 0)
    early[0] = product(second, 1) - product(here, 2)
    early[1] = product(fourth, 3)
    early[2] = product(second, 4)
    onward[...] = product(fourth, 5)
    for copy in rest:
        copy.wait()


def centre_body(middle, inverses, following, coarse, copies, held, sems):
    pieces = Pieces(sems)
    pieces.load(coarse, held)
    total = apply(from_four(middle), inverses[0])
    total -= apply(from_following(following), inverses[1])
    pieces.wait()
    total -= held[...]
    spread(copies, [part.astype(BF16) for part in own_and_partner(total)])


def onward_body(middle, begun, lifts, lifts_partner, totals, held, begun_held, sems):
    pieces = Pieces(sems)
    pieces.both(lifts.at[1], lifts_partner.at[1], held)
    pieces.load(begun, begun_held)
    full = from_four(middle)
    pieces.wait()
    total = begun_held[...] + apply(full, held[...])
    for i, part in enumerate(own_and_partner(total)):
        totals[i] = part.astype(BF16)


def reduced_body(
    middle, early, two, solve, sides, coarse, bundle, following,
    total, matrices, begun, kept, held, arrived, sides_held, early_held, sems,
):
    pieces = Pieces(sems)
    pieces.both(two.at[0, 1], bundle.at[3], held.at[0])
    pieces.both(solve.at[1, 2], bundle.at[12], held.at[1])
    pieces.load(following, arrived)
    pieces.load(early, early_held)
    load_sides(pieces, 0, sides, bundle, sides_held)
    pieces.both(solve.at[0, 2], bundle.at[9], matrices.at[0])
    pieces.both(solve.at[1, 1], bundle.at[11], matrices.at[1])
    pieces.load(coarse.at[0], kept)
    full = from_four(middle)
    pieces.wait()
    begun[0] = early_held[0]
    both = early_held[2] + apply(full, held[0])
    for i, part in enumerate(own_and_partner(both)):
        total[i] = sides_held[i].astype(F32) - part
    begun[1] = early_held[1] - apply(from_following(arrived), held[1])


def final_body(centre, matrices, begun, total, before, kept, given, sems):
    full = from_four(centre)
    chip, mine = lax.div(lax.axis_index("col"), 2), core()
    first = begun[0] - apply(full, matrices[0])
    last = begun[1] - apply(full, matrices[1])
    for i, out in enumerate((kept, given)):
        out[0] = own_and_partner(first)[i].astype(BF16)
        out[1] = centre[chip, mine if i == 0 else 1 - mine]
        out[2] = own_and_partner(last)[i].astype(BF16)
        out[3] = (total[i] - before[i].astype(F32)).astype(BF16)


def place_body(taken, coarse, kept, solved, reduced, sems):
    mine = core()
    solved[0] = coarse[...]
    for i in range(3):
        solved[i + 1, mine] = kept[i]
        solved[i + 1, 1 - mine] = taken[1 - mine, i]
    reduced[0, mine] = kept[3]
    reduced[0, 1 - mine] = taken[1 - mine, 3]


def steps(right_sides, coarse_solution, lift_one, solve_one, lift_two, solve_two):
    sides = right_sides.reshape(4, 2, HALF, WIDTH)
    coarse = coarse_solution.reshape(1, 2, HALF, WIDTH)
    packed = pack(sides, coarse)
    odd = lax.all_to_all(packed, "col", 0, 0)
    bundle, lifts = bundled(lift_one, lift_two, solve_one, solve_two, sides)
    lifts_next = passed_along(lifts, -1)
    bundle = from_partner(bundle)
    following = passed_along(odd[:, 2], -1)
    lifts_partner = from_partner(lifts_next)

    lift_matrices, begun = call(
        prepare_body,
        [(IN_VMEM, (2, *MERGED), BF16), (IN_VMEM, PAIR, BF16)],
        [],
        [lift_one, bundle, sides],
        copies=9,
    )
    (middle_copies,) = call(
        middle_body,
        [(IN_HBM, COPIES, BF16)],
        [odd, lift_matrices, begun],
        products=2,
    )
    middle = over_chips(middle_copies)
    flat = (HALF, 2 * WIDTH)
    inverses, coarse_begun, early, onward_begun = call(
        early_body,
        [
            (IN_VMEM, (2, *MERGED), BF16),
            (IN_HBM, flat, F32),
            (IN_HBM, (3, *flat), F32),
            (IN_HBM, flat, F32),
        ],
        [odd],
        [lift_one, solve_one, solve_two, bundle, lifts_next],
        [((6, *MERGED), BF16)],
        copies=16,
        products=6,
        free=[lifts_partner],
    )
    (centre_copies,) = call(
        centre_body,
        [(IN_HBM, COPIES, BF16)],
        [middle, inverses, following],
        [coarse_begun],
        [(flat, F32)],
        copies=1,
        products=2,
    )
    centre = over_chips(centre_copies)
    (onward,) = call(
        onward_body,
        [(IN_VMEM, PAIR, BF16)],
        [middle],
        [onward_begun, lifts_next],
        [(MERGED, BF16), (flat, F32)],
        free=[lifts_partner],
        copies=3,
    )
    before = passed_along(onward, 1)
    total, solve_matrices, ends_begun, coarse_kept = call(
        reduced_body,
        [
            (IN_VMEM, PAIR, F32),
            (IN_VMEM, (2, *MERGED), BF16),
            (IN_VMEM, (2, *flat), F32),
            (IN_VMEM, PAIR, BF16),
        ],
        [middle],
        [early, lift_two, solve_one, sides, coarse, bundle],
        [
            ((2, *MERGED), BF16),
            ((8, HALF, WIDTH), BF16),
            (PAIR, BF16),
            ((3, *flat), F32),
        ],
        copies=16,
        products=3,
        free=[following],
    )
    kept, given = call(
        final_body,
        [(IN_VMEM, (4, HALF, WIDTH), BF16)] * 2,
        [centre, solve_matrices, ends_begun, total, before],
        products=2,
    )
    cores = [[i, i + 1] for i in range(0, lax.axis_size("col"), 2)]
    taken = lax.all_gather(given, "col", axis=0, axis_index_groups=cores)
    solved, reduced = call(
        place_body,
        [
            (IN_HBM, (4, 2, HALF, WIDTH), BF16),
            (IN_HBM, (1, 2, HALF, WIDTH), BF16),
        ],
        [taken, coarse_kept, kept],
    )
    return solved.reshape(4, ROWS, WIDTH), reduced.reshape(1, ROWS, WIDTH)


def solution(mesh):
    return jax.shard_map(
        steps,
        mesh=mesh,
        in_specs=(
            P("rad", None, "col"),
            P("rad", None, "col"),
            P("rad", None, "col", None),
            P("rad", None, "col", None),
            P("rad", None, "col", None),
            P("rad", None, "col", None),
        ),
        out_specs=(P("rad", None, "col"), P("rad", None, "col")),
        check_vma=False,
    )
```

```python
import jax
import jax.numpy as jnp
from jax import lax
from jax.experimental import pallas as pl
from jax.experimental.pallas import tpu as pltpu
from jax.sharding import PartitionSpec as P


ANY = pl.BlockSpec(memory_space=pl.ANY)
ROWS = 384
HALF = 192
WIDTH = 128
BF16 = jnp.bfloat16
F32 = jnp.float32
VMEM = pl.BlockSpec(memory_space=pltpu.VMEM)
HBM = pl.BlockSpec(memory_space=pltpu.HBM)


def chips_of(peers):
    return [[i for i in range(peers) if i % 2 == core] for core in range(2)]


def over_chips(copies):
    groups = chips_of(lax.axis_size("col"))
    return lax.all_to_all(copies, "col", 0, 0, axis_index_groups=groups)


def from_partner(array):
    peers = lax.axis_size("col")
    return lax.ppermute(array, "col", [(i, i ^ 1) for i in range(peers)])


def passed_along(array, by):
    peers = lax.axis_size("rad")
    pairs = [(i, i + by) for i in range(peers) if 0 <= i + by < peers]
    return lax.ppermute(array, "rad", pairs)


def apply(vector, matrix):
    return lax.dot_general(
        vector, matrix, (((1,), (1,)), ((), ())), preferred_element_type=F32
    )


def core():
    return lax.rem(lax.axis_index("col"), 2)


class Pieces:
    def __init__(self, sems):
        self.sems, self.copies = sems, []

    def load(self, source, held):
        sem = self.sems.at[len(self.copies)]
        copy = pltpu.make_async_copy(source, held, sem)
        copy.start()
        self.copies.append(copy)
        return copy

    def both(self, own, partner, held):
        return (
            self.load(own, held.at[pl.ds(0, WIDTH)]),
            self.load(partner, held.at[pl.ds(WIDTH, WIDTH)]),
        )

    def wait(self):
        for copy in self.copies:
            copy.wait()


def call(body, outs, whole, parts=(), scratch=(), copies=0, products=1, free=()):
    return pl.pallas_call(
        body,
        out_shape=[space(shape, dtype) for space, shape, dtype in outs],
        in_specs=[VMEM] * len(whole)
        + [HBM] * len(parts)
        + [ANY] * len(free),
        out_specs=[VMEM] * len(outs),
        scratch_shapes=[pltpu.VMEM(*one) for one in scratch]
        + [pltpu.SemaphoreType.DMA((max(copies, 1),))],
        compiler_params=pltpu.CompilerParams(vmem_limit_bytes=12 << 20),
        cost_estimate=pl.CostEstimate(
            flops=products * 2 * ROWS * 1024 * WIDTH,
            bytes_accessed=products * 1000000,
            transcendentals=0,
        ),
    )(
        *[pltpu.with_memory_space_constraint(x, pltpu.VMEM) for x in whole],
        *[pltpu.with_memory_space_constraint(x, pltpu.HBM) for x in parts],
        *free,
    )


IN_VMEM, IN_HBM = pltpu.VMEM, pltpu.HBM
PAIR = (2, HALF, WIDTH)
COPIES = (4, 2, HALF, WIDTH)
MERGED = (2 * WIDTH, 1024)
STRIPS, STRIP = 4, 48


def from_eight(blocks, which):
    return jnp.concatenate([blocks[peer, which] for peer in range(8)], axis=1)


def from_four(blocks, at=0):
    return jnp.concatenate(
        [blocks[chip, at + side] for chip in range(4) for side in range(2)], axis=1
    )


def pack_body(sides, coarse, packed, held, arrived, sent):
    arrays = [sides.at[1], sides.at[3], coarse.at[0]]
    loads = [
        pltpu.make_async_copy(array, held.at[i], arrived.at[i])
        for i, array in enumerate(arrays)
    ]
    for load in loads:
        load.start()
    stores = []
    for i, load in enumerate(loads):
        load.wait()
        for peer in range(8):
            store = pltpu.make_async_copy(
                held.at[i, peer % 2], packed.at[peer, i], sent.at[i, peer]
            )
            store.start()
            stores.append(store)
    for store in stores:
        store.wait()


def pack(sides, coarse):
    return pl.pallas_call(
        pack_body,
        out_shape=pltpu.HBM((8, 3, HALF, WIDTH), BF16),
        in_specs=[HBM, HBM],
        out_specs=HBM,
        scratch_shapes=[
            pltpu.VMEM((3, 2, HALF, WIDTH), BF16),
            pltpu.SemaphoreType.DMA((3,)),
            pltpu.SemaphoreType.DMA((3, 8)),
        ],
        compiler_params=pltpu.CompilerParams(vmem_limit_bytes=4 << 20),
    )(
        pltpu.with_memory_space_constraint(sides, pltpu.HBM),
        pltpu.with_memory_space_constraint(coarse, pltpu.HBM),
    )


def own_and_partner(total):
    return total[:, :WIDTH], total[:, WIDTH:]


def spread(copies, results, at=0):
    mine = core()
    for chip in range(4):
        copies[chip, at + mine] = results[0]
        copies[chip, at + 1 - mine] = results[1]


def bundle_body(
    one, two, solve_one, solve_two, sides, coarse, first, second, lifts,
    first_held, held, lifts_held, arrived, sent,
):
    other = 1 - core()
    incoming, outgoing = Pieces(arrived), Pieces(sent)
    pair, triple = pl.ds(0, 2), pl.ds(2, 3)
    rows = []
    for j in range(3 * STRIPS):
        half = coarse.at[0, other] if j < STRIPS else sides.at[2 * (j // STRIPS - 1), other]
        strip = half.at[pl.ds(STRIP * (j % STRIPS), STRIP)]
        rows.append(incoming.load(strip, strip_of(first_held, j)))
    groups = (
        (one.at[1], first_held.at[pair], first.at[pair]),
        (one.at[0, 1], held.at[0], second.at[0]),
        (two.at[0, 1], held.at[1], second.at[1]),
        (solve_two.at[0], held.at[triple], second.at[triple]),
        (solve_one.at[0], held.at[pl.ds(5, 3)], second.at[pl.ds(5, 3)]),
        (solve_one.at[1], held.at[pl.ds(8, 3)], second.at[pl.ds(8, 3)]),
        (one.at[0, 0], lifts_held.at[0], lifts.at[0]),
        (two.at[0, 0], lifts_held.at[1], lifts.at[1]),
    )
    loads = [incoming.load(source, place) for source, place, _ in groups]
    for row in rows:
        row.wait()
    used = pl.ds(0, 2 * STRIP)
    outgoing.load(first_held.at[2, used], first.at[2, used])
    for load, (_, place, target) in zip(loads, groups):
        load.wait()
        outgoing.load(place, target)
    outgoing.wait()


def strip_of(bundle, j):
    row, column = (0, j) if j < 2 * STRIPS else (1, j - 2 * STRIPS)
    return bundle.at[2, pl.ds(STRIP * row, STRIP), pl.ds(WIDTH * column, WIDTH)]


def bundled(*arrays):
    shapes = [(3, WIDTH, 1024), (11, WIDTH, 1024), (2, WIDTH, 1024)]
    return pl.pallas_call(
        bundle_body,
        out_shape=[pltpu.HBM(shape, BF16) for shape in shapes],
        in_specs=[HBM] * len(arrays),
        out_specs=[HBM] * 3,
        scratch_shapes=[pltpu.VMEM(shape, BF16) for shape in shapes]
        + [
            pltpu.SemaphoreType.DMA((8 + 3 * STRIPS,)),
            pltpu.SemaphoreType.DMA((9,)),
        ],
        compiler_params=pltpu.CompilerParams(vmem_limit_bytes=12 << 20),
        cost_estimate=pl.CostEstimate(
            flops=0, bytes_accessed=9000000, transcendentals=0
        ),
    )(*[pltpu.with_memory_space_constraint(x, pltpu.HBM) for x in arrays])


def load_half(pieces, own, bundle, which, held):
    pieces.load(own, held.at[0])
    for j in range(STRIPS):
        place = held.at[1, pl.ds(STRIP * j, STRIP)]
        pieces.load(strip_of(bundle, STRIPS * which + j), place)


def prepare_body(one, bundle, sides, coarse, matrices, begun, coarse_pair, sems):
    pieces, mine = Pieces(sems), core()
    load_half(pieces, coarse.at[0, mine], bundle, 0, coarse_pair)
    for i in range(2):
        pieces.both(one.at[1, i], bundle.at[i], matrices.at[i])
    load_half(pieces, sides.at[2, mine], bundle, 2, begun)
    pieces.wait()


def middle_body(odd, matrices, begun, following, copies, sems):
    total = apply(from_eight(odd, 0), matrices[0])
    total += apply(from_eight(odd, 1), matrices[1])
    spread(
        copies,
        [
            (begun[i].astype(F32) - part).astype(BF16)
            for i, part in enumerate(own_and_partner(total))
        ],
    )
    spread(copies, [following[0], following[1]], 2)


def early_body(
    odd, one, solve, last, bundle, inverses, coarse, early, onward, held, sems
):
    pieces = Pieces(sems)
    waits = [
        pieces.both(own, partner, held.at[i])
        for i, (own, partner) in enumerate(
            (
                (last.at[0, 1], bundle.at[3]),
                (solve.at[0, 0], bundle.at[5]),
                (solve.at[0, 1], bundle.at[6]),
                (solve.at[1, 0], bundle.at[8]),
                (one.at[0, 1], bundle.at[0]),
            )
        )
    ]
    rest = pieces.both(last.at[0, 0], bundle.at[2], inverses.at[0])
    rest += pieces.both(last.at[0, 2], bundle.at[4], inverses.at[1])

    def product(vector, i):
        for copy in waits[i]:
            copy.wait()
        return apply(vector, held[i])

    second, fourth, here = (from_eight(odd, i) for i in range(3))
    onward[...] = fourth
    coarse[...] = product(here, 0)
    early[0] = product(second, 1) - product(here, 2)
    early[1] = product(fourth, 3)
    early[2] = product(second, 4)
    for copy in rest:
        copy.wait()


def centre_body(gathered, inverses, coarse, copies, sems):
    total = apply(from_four(gathered), inverses[0])
    total -= apply(from_four(gathered, 2), inverses[1]) + coarse[...]
    spread(copies, [part.astype(BF16) for part in own_and_partner(total)])


def onward_body(
    gathered, fourth, lifts, lifts_partner, totals, held, fourth_held, sems
):
    pieces = Pieces(sems)
    for i in range(2):
        pieces.both(lifts.at[i], lifts_partner.at[i], held.at[i])
    pieces.load(fourth, fourth_held)
    full = from_four(gathered)
    pieces.wait()
    total = apply(fourth_held[...], held[0]) + apply(full, held[1])
    for i, part in enumerate(own_and_partner(total)):
        totals[i] = part.astype(BF16)


def reduced_body(
    gathered, early, two, solve, sides, coarse, first, second,
    total, matrices, begun, kept, held, sides_held, early_held, sems,
):
    pieces = Pieces(sems)
    pieces.both(two.at[0, 1], second.at[1], held.at[0])
    pieces.both(solve.at[1, 2], second.at[10], held.at[1])
    pieces.load(early, early_held)
    load_half(pieces, sides.at[0, core()], first, 1, sides_held)
    pieces.both(solve.at[0, 2], second.at[7], matrices.at[0])
    pieces.both(solve.at[1, 1], second.at[9], matrices.at[1])
    pieces.load(coarse.at[0], kept)
    pieces.wait()
    begun[0] = early_held[0]
    both = early_held[2] + apply(from_four(gathered), held[0])
    for i, part in enumerate(own_and_partner(both)):
        total[i] = sides_held[i].astype(F32) - part
    begun[1] = early_held[1] - apply(from_four(gathered, 2), held[1])


def final_body(centre, matrices, begun, total, before, kept, given, sems):
    full = from_four(centre)
    chip, mine = lax.div(lax.axis_index("col"), 2), core()
    first = begun[0] - apply(full, matrices[0])
    last = begun[1] - apply(full, matrices[1])
    for i, out in enumerate((kept, given)):
        out[0] = own_and_partner(first)[i].astype(BF16)
        out[1] = centre[chip, mine if i == 0 else 1 - mine]
        out[2] = own_and_partner(last)[i].astype(BF16)
        out[3] = (total[i] - before[i].astype(F32)).astype(BF16)


def place_body(taken, coarse, kept, solved, reduced, sems):
    mine = core()
    solved[0] = coarse[...]
    for i in range(3):
        solved[i + 1, mine] = kept[i]
        solved[i + 1, 1 - mine] = taken[1 - mine, i]
    reduced[0, mine] = kept[3]
    reduced[0, 1 - mine] = taken[1 - mine, 3]


def steps(right_sides, coarse_solution, lift_one, solve_one, lift_two, solve_two):
    sides = right_sides.reshape(4, 2, HALF, WIDTH)
    coarse = coarse_solution.reshape(1, 2, HALF, WIDTH)
    packed = pack(sides, coarse)
    odd = lax.all_to_all(packed, "col", 0, 0)
    first, second, lifts = bundled(
        lift_one, lift_two, solve_one, solve_two, sides, coarse
    )
    first = from_partner(first)
    second = from_partner(second)
    lift_matrices, begun, coarse_pair = call(
        prepare_body,
        [
            (IN_VMEM, (2, *MERGED), BF16),
            (IN_VMEM, PAIR, BF16),
            (IN_VMEM, PAIR, BF16),
        ],
        [],
        [lift_one, first, sides, coarse],
        copies=14,
    )
    following = passed_along(coarse_pair, -1)
    lifts_next = passed_along(lifts, -1)
    lifts_partner = from_partner(lifts_next)
    (middle_copies,) = call(
        middle_body,
        [(IN_HBM, (4, 4, HALF, WIDTH), BF16)],
        [odd, lift_matrices, begun, following],
        products=2,
    )
    gathered = over_chips(middle_copies)
    flat = (HALF, 2 * WIDTH)
    inverses, coarse_begun, early, fourth = call(
        early_body,
        [
            (IN_VMEM, (2, *MERGED), BF16),
            (IN_VMEM, flat, F32),
            (IN_HBM, (3, *flat), F32),
            (IN_HBM, (HALF, 1024), BF16),
        ],
        [odd],
        [lift_one, solve_one, solve_two, second],
        [((5, *MERGED), BF16)],
        copies=14,
        products=5,
    )
    (centre_copies,) = call(
        centre_body,
        [(IN_HBM, COPIES, BF16)],
        [gathered, inverses, coarse_begun],
        products=2,
    )
    centre = over_chips(centre_copies)
    (onward,) = call(
        onward_body,
        [(IN_VMEM, PAIR, BF16)],
        [gathered],
        [fourth, lifts_next],
        [((2, *MERGED), BF16), ((HALF, 1024), BF16)],
        free=[lifts_partner],
        copies=5,
    )
    before = passed_along(onward, 1)
    total, solve_matrices, ends_begun, coarse_kept = call(
        reduced_body,
        [
            (IN_VMEM, PAIR, F32),
            (IN_VMEM, (2, *MERGED), BF16),
            (IN_VMEM, (2, *flat), F32),
            (IN_VMEM, PAIR, BF16),
        ],
        [gathered],
        [early, lift_two, solve_one, sides, coarse, first, second],
        [((2, *MERGED), BF16), (PAIR, BF16), ((3, *flat), F32)],
        copies=15,
        products=3,
    )
    kept, given = call(
        final_body,
        [(IN_VMEM, (4, HALF, WIDTH), BF16)] * 2,
        [centre, solve_matrices, ends_begun, total, before],
        products=2,
    )
    cores = [[i, i + 1] for i in range(0, lax.axis_size("col"), 2)]
    taken = lax.all_gather(given, "col", axis=0, axis_index_groups=cores)
    solved, reduced = call(
        place_body,
        [
            (IN_HBM, (4, 2, HALF, WIDTH), BF16),
            (IN_HBM, (1, 2, HALF, WIDTH), BF16),
        ],
        [taken, coarse_kept, kept],
    )
    return solved.reshape(4, ROWS, WIDTH), reduced.reshape(1, ROWS, WIDTH)


def solution(mesh):
    return jax.shard_map(
        steps,
        mesh=mesh,
        in_specs=(
            P("rad", None, "col"),
            P("rad", None, "col"),
            P("rad", None, "col", None),
            P("rad", None, "col", None),
            P("rad", None, "col", None),
            P("rad", None, "col", None),
        ),
        out_specs=(P("rad", None, "col"), P("rad", None, "col")),
        check_vma=False,
    )
```

```python
import jax
import jax.numpy as jnp
from jax import lax
from jax.experimental import pallas as pl
from jax.experimental.pallas import tpu as pltpu
from jax.sharding import PartitionSpec as P


ANY = pl.BlockSpec(memory_space=pl.ANY)
ROWS = 384
HALF = 192
WIDTH = 128
BF16 = jnp.bfloat16
F32 = jnp.float32
VMEM = pl.BlockSpec(memory_space=pltpu.VMEM)
HBM = pl.BlockSpec(memory_space=pltpu.HBM)


def chips_of(peers):
    return [[i for i in range(peers) if i % 2 == core] for core in range(2)]


def over_chips(copies):
    groups = chips_of(lax.axis_size("col"))
    return lax.all_to_all(copies, "col", 0, 0, axis_index_groups=groups)


def from_partner(array):
    peers = lax.axis_size("col")
    return lax.ppermute(array, "col", [(i, i ^ 1) for i in range(peers)])


def passed_along(array, by):
    peers = lax.axis_size("rad")
    pairs = [(i, i + by) for i in range(peers) if 0 <= i + by < peers]
    return lax.ppermute(array, "rad", pairs)


def apply(vector, matrix):
    return lax.dot_general(
        vector, matrix, (((1,), (1,)), ((), ())), preferred_element_type=F32
    )


def core():
    return lax.rem(lax.axis_index("col"), 2)


class Pieces:
    def __init__(self, sems):
        self.sems, self.copies = sems, []

    def load(self, source, held):
        sem = self.sems.at[len(self.copies)]
        copy = pltpu.make_async_copy(source, held, sem)
        copy.start()
        self.copies.append(copy)
        return copy

    def both(self, own, partner, held):
        return (
            self.load(own, held.at[pl.ds(0, WIDTH)]),
            self.load(partner, held.at[pl.ds(WIDTH, WIDTH)]),
        )

    def wait(self):
        for copy in self.copies:
            copy.wait()


def call(body, outs, whole, parts=(), scratch=(), copies=0, products=1, free=()):
    return pl.pallas_call(
        body,
        out_shape=[space(shape, dtype) for space, shape, dtype in outs],
        in_specs=[VMEM] * len(whole)
        + [HBM] * len(parts)
        + [ANY] * len(free),
        out_specs=[VMEM] * len(outs),
        scratch_shapes=[pltpu.VMEM(*one) for one in scratch]
        + [pltpu.SemaphoreType.DMA((max(copies, 1),))],
        compiler_params=pltpu.CompilerParams(vmem_limit_bytes=12 << 20),
        cost_estimate=pl.CostEstimate(
            flops=products * 2 * ROWS * 1024 * WIDTH,
            bytes_accessed=products * 1000000,
            transcendentals=0,
        ),
    )(
        *[pltpu.with_memory_space_constraint(x, pltpu.VMEM) for x in whole],
        *[pltpu.with_memory_space_constraint(x, pltpu.HBM) for x in parts],
        *free,
    )


IN_VMEM, IN_HBM = pltpu.VMEM, pltpu.HBM
PAIR = (2, HALF, WIDTH)
COPIES = (4, 2, HALF, WIDTH)
MERGED = (2 * WIDTH, 1024)
STRIPS, STRIP = 4, 48


def from_eight(blocks, which):
    return jnp.concatenate([blocks[peer, which] for peer in range(8)], axis=1)


def from_four(blocks, at=0):
    return jnp.concatenate(
        [blocks[chip, at + side] for chip in range(4) for side in range(2)], axis=1
    )


def pack_body(sides, coarse, packed, held, arrived, sent):
    arrays = [sides.at[1], sides.at[3], coarse.at[0]]
    loads = [
        pltpu.make_async_copy(array, held.at[i], arrived.at[i])
        for i, array in enumerate(arrays)
    ]
    for load in loads:
        load.start()
    stores = []
    for i, load in enumerate(loads):
        load.wait()
        for peer in range(8):
            store = pltpu.make_async_copy(
                held.at[i, peer % 2], packed.at[peer, i], sent.at[i, peer]
            )
            store.start()
            stores.append(store)
    for store in stores:
        store.wait()


def pack(sides, coarse):
    return pl.pallas_call(
        pack_body,
        out_shape=pltpu.HBM((8, 3, HALF, WIDTH), BF16),
        in_specs=[HBM, HBM],
        out_specs=HBM,
        scratch_shapes=[
            pltpu.VMEM((3, 2, HALF, WIDTH), BF16),
            pltpu.SemaphoreType.DMA((3,)),
            pltpu.SemaphoreType.DMA((3, 8)),
        ],
        compiler_params=pltpu.CompilerParams(vmem_limit_bytes=4 << 20),
    )(
        pltpu.with_memory_space_constraint(sides, pltpu.HBM),
        pltpu.with_memory_space_constraint(coarse, pltpu.HBM),
    )


def own_and_partner(total):
    return total[:, :WIDTH], total[:, WIDTH:]


def spread(copies, results, at=0):
    mine = core()
    for chip in range(4):
        copies[chip, at + mine] = results[0]
        copies[chip, at + 1 - mine] = results[1]


def bundle_body(
    one, two, solve_one, solve_two, sides, coarse, first, second, lifts,
    first_held, held, lifts_held, arrived, sent,
):
    other = 1 - core()
    incoming, outgoing = Pieces(arrived), Pieces(sent)
    pair, triple = pl.ds(0, 2), pl.ds(2, 3)
    rows = []
    for j in range(3 * STRIPS):
        half = coarse.at[0, other] if j < STRIPS else sides.at[2 * (j // STRIPS - 1), other]
        strip = half.at[pl.ds(STRIP * (j % STRIPS), STRIP)]
        rows.append(incoming.load(strip, strip_of(first_held, j)))
    groups = (
        (one.at[1], first_held.at[pair], first.at[pair]),
        (one.at[0, 1], held.at[0], second.at[0]),
        (two.at[0, 1], held.at[1], second.at[1]),
        (solve_two.at[0], held.at[triple], second.at[triple]),
        (solve_one.at[0], held.at[pl.ds(5, 3)], second.at[pl.ds(5, 3)]),
        (solve_one.at[1], held.at[pl.ds(8, 3)], second.at[pl.ds(8, 3)]),
        (one.at[0, 0], lifts_held.at[0], lifts.at[0]),
        (two.at[0, 0], lifts_held.at[1], lifts.at[1]),
    )
    loads = [incoming.load(source, place) for source, place, _ in groups]
    for row in rows:
        row.wait()
    used = pl.ds(0, 2 * STRIP)
    outgoing.load(first_held.at[2, used], first.at[2, used])
    for load, (_, place, target) in zip(loads, groups):
        load.wait()
        outgoing.load(place, target)
    outgoing.wait()


def strip_of(bundle, j):
    row, column = (0, j) if j < 2 * STRIPS else (1, j - 2 * STRIPS)
    return bundle.at[2, pl.ds(STRIP * row, STRIP), pl.ds(WIDTH * column, WIDTH)]


def bundled(*arrays):
    shapes = [(3, WIDTH, 1024), (11, WIDTH, 1024), (2, WIDTH, 1024)]
    return pl.pallas_call(
        bundle_body,
        out_shape=[pltpu.HBM(shape, BF16) for shape in shapes],
        in_specs=[HBM] * len(arrays),
        out_specs=[HBM] * 3,
        scratch_shapes=[pltpu.VMEM(shape, BF16) for shape in shapes]
        + [
            pltpu.SemaphoreType.DMA((8 + 3 * STRIPS,)),
            pltpu.SemaphoreType.DMA((9,)),
        ],
        compiler_params=pltpu.CompilerParams(vmem_limit_bytes=12 << 20),
        cost_estimate=pl.CostEstimate(
            flops=0, bytes_accessed=9000000, transcendentals=0
        ),
    )(*[pltpu.with_memory_space_constraint(x, pltpu.HBM) for x in arrays])


def load_half(pieces, own, bundle, which, held):
    pieces.load(own, held.at[0])
    for j in range(STRIPS):
        place = held.at[1, pl.ds(STRIP * j, STRIP)]
        pieces.load(strip_of(bundle, STRIPS * which + j), place)


def prepare_body(one, sides, coarse, bundle, matrices, begun, coarse_pair, sems):
    pieces, mine = Pieces(sems), core()
    load_half(pieces, coarse.at[0, mine], bundle, 0, coarse_pair)
    for i in range(2):
        pieces.both(one.at[1, i], bundle.at[i], matrices.at[i])
    for i in range(2):
        load_half(pieces, sides.at[2 * i, mine], bundle, 1 + i, begun.at[i])
    pieces.wait()


def middle_body(odd, matrices, begun, following, copies, sems):
    total = apply(from_eight(odd, 0), matrices[0])
    total += apply(from_eight(odd, 1), matrices[1])
    spread(
        copies,
        [
            (begun[1, i].astype(F32) - part).astype(BF16)
            for i, part in enumerate(own_and_partner(total))
        ],
    )
    spread(copies, [following[0], following[1]], 2)


def early_body(
    odd, one, solve, last, bundle, inverses, coarse, early, onward, held, sems
):
    pieces = Pieces(sems)
    waits = [
        pieces.both(own, partner, held.at[i])
        for i, (own, partner) in enumerate(
            (
                (last.at[0, 1], bundle.at[3]),
                (solve.at[0, 0], bundle.at[5]),
                (solve.at[0, 1], bundle.at[6]),
                (solve.at[1, 0], bundle.at[8]),
                (one.at[0, 1], bundle.at[0]),
            )
        )
    ]
    rest = pieces.both(last.at[0, 0], bundle.at[2], inverses.at[0])
    rest += pieces.both(last.at[0, 2], bundle.at[4], inverses.at[1])

    def product(vector, i):
        for copy in waits[i]:
            copy.wait()
        return apply(vector, held[i])

    second, fourth, here = (from_eight(odd, i) for i in range(3))
    onward[...] = fourth
    coarse[...] = product(here, 0)
    early[0] = product(second, 1) - product(here, 2)
    early[1] = product(fourth, 3)
    early[2] = product(second, 4)
    for copy in rest:
        copy.wait()


def centre_body(gathered, inverses, coarse, copies, sems):
    total = apply(from_four(gathered), inverses[0])
    total -= apply(from_four(gathered, 2), inverses[1]) + coarse[...]
    spread(copies, [part.astype(BF16) for part in own_and_partner(total)])


def onward_body(
    gathered, fourth, lifts, lifts_partner, totals, held, fourth_held, sems
):
    pieces = Pieces(sems)
    for i in range(2):
        pieces.both(lifts.at[i], lifts_partner.at[i], held.at[i])
    pieces.load(fourth, fourth_held)
    full = from_four(gathered)
    pieces.wait()
    total = apply(fourth_held[...], held[0]) + apply(full, held[1])
    for i, part in enumerate(own_and_partner(total)):
        totals[i] = part.astype(BF16)


def reduced_body(
    gathered, early, two, solve, coarse, second, sides_begun,
    total, matrices, begun, kept, held, sides_held, early_held, sems,
):
    pieces = Pieces(sems)
    pieces.both(two.at[0, 1], second.at[1], held.at[0])
    pieces.both(solve.at[1, 2], second.at[10], held.at[1])
    pieces.load(early, early_held)
    pieces.load(sides_begun.at[0], sides_held)
    pieces.both(solve.at[0, 2], second.at[7], matrices.at[0])
    pieces.both(solve.at[1, 1], second.at[9], matrices.at[1])
    pieces.load(coarse.at[0], kept)
    pieces.wait()
    begun[0] = early_held[0]
    both = early_held[2] + apply(from_four(gathered), held[0])
    for i, part in enumerate(own_and_partner(both)):
        total[i] = sides_held[i].astype(F32) - part
    begun[1] = early_held[1] - apply(from_four(gathered, 2), held[1])


def final_body(centre, matrices, begun, total, before, kept, given, sems):
    full = from_four(centre)
    chip, mine = lax.div(lax.axis_index("col"), 2), core()
    first = begun[0] - apply(full, matrices[0])
    last = begun[1] - apply(full, matrices[1])
    for i, out in enumerate((kept, given)):
        out[0] = own_and_partner(first)[i].astype(BF16)
        out[1] = centre[chip, mine if i == 0 else 1 - mine]
        out[2] = own_and_partner(last)[i].astype(BF16)
        out[3] = (total[i] - before[i].astype(F32)).astype(BF16)


def place_body(taken, coarse, kept, solved, reduced, sems):
    mine = core()
    solved[0] = coarse[...]
    for i in range(3):
        solved[i + 1, mine] = kept[i]
        solved[i + 1, 1 - mine] = taken[1 - mine, i]
    reduced[0, mine] = kept[3]
    reduced[0, 1 - mine] = taken[1 - mine, 3]


def steps(right_sides, coarse_solution, lift_one, solve_one, lift_two, solve_two):
    sides = right_sides.reshape(4, 2, HALF, WIDTH)
    coarse = coarse_solution.reshape(1, 2, HALF, WIDTH)
    packed = pack(sides, coarse)
    odd = lax.all_to_all(packed, "col", 0, 0)
    first, second, lifts = bundled(
        lift_one, lift_two, solve_one, solve_two, sides, coarse
    )
    first = from_partner(first)
    second = from_partner(second)
    lift_matrices, begun, coarse_pair = call(
        prepare_body,
        [
            (IN_VMEM, (2, *MERGED), BF16),
            (IN_VMEM, (2, *PAIR), BF16),
            (IN_VMEM, PAIR, BF16),
        ],
        [],
        [lift_one, sides, coarse],
        free=[first],
        copies=19,
    )
    following = passed_along(coarse_pair, -1)
    lifts_next = passed_along(lifts, -1)
    lifts_partner = from_partner(lifts_next)
    (middle_copies,) = call(
        middle_body,
        [(IN_HBM, (4, 4, HALF, WIDTH), BF16)],
        [odd, lift_matrices, begun, following],
        products=2,
    )
    gathered = over_chips(middle_copies)
    flat = (HALF, 2 * WIDTH)
    inverses, coarse_begun, early, fourth = call(
        early_body,
        [
            (IN_VMEM, (2, *MERGED), BF16),
            (IN_VMEM, flat, F32),
            (IN_HBM, (3, *flat), F32),
            (IN_HBM, (HALF, 1024), BF16),
        ],
        [odd],
        [lift_one, solve_one, solve_two, second],
        [((5, *MERGED), BF16)],
        copies=14,
        products=5,
    )
    (centre_copies,) = call(
        centre_body,
        [(IN_HBM, COPIES, BF16)],
        [gathered, inverses, coarse_begun],
        products=2,
    )
    centre = over_chips(centre_copies)
    (onward,) = call(
        onward_body,
        [(IN_VMEM, PAIR, BF16)],
        [gathered],
        [fourth, lifts_next],
        [((2, *MERGED), BF16), ((HALF, 1024), BF16)],
        free=[lifts_partner],
        copies=5,
    )
    before = passed_along(onward, 1)
    total, solve_matrices, ends_begun, coarse_kept = call(
        reduced_body,
        [
            (IN_VMEM, PAIR, F32),
            (IN_VMEM, (2, *MERGED), BF16),
            (IN_VMEM, (2, *flat), F32),
            (IN_VMEM, PAIR, BF16),
        ],
        [gathered],
        [early, lift_two, solve_one, coarse, second],
        [((2, *MERGED), BF16), (PAIR, BF16), ((3, *flat), F32)],
        free=[begun],
        copies=11,
        products=3,
    )
    kept, given = call(
        final_body,
        [(IN_VMEM, (4, HALF, WIDTH), BF16)] * 2,
        [centre, solve_matrices, ends_begun, total, before],
        products=2,
    )
    cores = [[i, i + 1] for i in range(0, lax.axis_size("col"), 2)]
    taken = lax.all_gather(given, "col", axis=0, axis_index_groups=cores)
    solved, reduced = call(
        place_body,
        [
            (IN_HBM, (4, 2, HALF, WIDTH), BF16),
            (IN_HBM, (1, 2, HALF, WIDTH), BF16),
        ],
        [taken, coarse_kept, kept],
    )
    return solved.reshape(4, ROWS, WIDTH), reduced.reshape(1, ROWS, WIDTH)


def solution(mesh):
    return jax.shard_map(
        steps,
        mesh=mesh,
        in_specs=(
            P("rad", None, "col"),
            P("rad", None, "col"),
            P("rad", None, "col", None),
            P("rad", None, "col", None),
            P("rad", None, "col", None),
            P("rad", None, "col", None),
        ),
        out_specs=(P("rad", None, "col"), P("rad", None, "col")),
        check_vma=False,
    )
```

```python
import jax
import jax.numpy as jnp
from jax import lax
from jax.experimental import pallas as pl
from jax.experimental.pallas import tpu as pltpu
from jax.sharding import PartitionSpec as P


ANY = pl.BlockSpec(memory_space=pl.ANY)
ROWS = 384
HALF = 192
WIDTH = 128
BF16 = jnp.bfloat16
F32 = jnp.float32
VMEM = pl.BlockSpec(memory_space=pltpu.VMEM)
HBM = pl.BlockSpec(memory_space=pltpu.HBM)


def chips_of(peers):
    return [[i for i in range(peers) if i % 2 == core] for core in range(2)]


def over_chips(copies):
    groups = chips_of(lax.axis_size("col"))
    return lax.all_to_all(copies, "col", 0, 0, axis_index_groups=groups)


def from_partner(array):
    peers = lax.axis_size("col")
    return lax.ppermute(array, "col", [(i, i ^ 1) for i in range(peers)])


def passed_along(array, by):
    peers = lax.axis_size("rad")
    pairs = [(i, i + by) for i in range(peers) if 0 <= i + by < peers]
    return lax.ppermute(array, "rad", pairs)


def apply(vector, matrix):
    return lax.dot_general(
        vector, matrix, (((1,), (1,)), ((), ())), preferred_element_type=F32
    )


def core():
    return lax.rem(lax.axis_index("col"), 2)


class Pieces:
    def __init__(self, sems):
        self.sems, self.copies = sems, []

    def load(self, source, held):
        sem = self.sems.at[len(self.copies)]
        copy = pltpu.make_async_copy(source, held, sem)
        copy.start()
        self.copies.append(copy)
        return copy

    def both(self, own, partner, held):
        return (
            self.load(own, held.at[pl.ds(0, WIDTH)]),
            self.load(partner, held.at[pl.ds(WIDTH, WIDTH)]),
        )

    def wait(self):
        for copy in self.copies:
            copy.wait()


def call(body, outs, whole, parts=(), scratch=(), copies=0, products=1, free=()):
    return pl.pallas_call(
        body,
        out_shape=[space(shape, dtype) for space, shape, dtype in outs],
        in_specs=[VMEM] * len(whole)
        + [HBM] * len(parts)
        + [ANY] * len(free),
        out_specs=[VMEM] * len(outs),
        scratch_shapes=[pltpu.VMEM(*one) for one in scratch]
        + [pltpu.SemaphoreType.DMA((max(copies, 1),))],
        compiler_params=pltpu.CompilerParams(vmem_limit_bytes=12 << 20),
        cost_estimate=pl.CostEstimate(
            flops=products * 2 * ROWS * 1024 * WIDTH,
            bytes_accessed=products * 1000000,
            transcendentals=0,
        ),
    )(
        *[pltpu.with_memory_space_constraint(x, pltpu.VMEM) for x in whole],
        *[pltpu.with_memory_space_constraint(x, pltpu.HBM) for x in parts],
        *free,
    )


IN_VMEM, IN_HBM = pltpu.VMEM, pltpu.HBM
PAIR = (2, HALF, WIDTH)
COPIES = (4, 2, HALF, WIDTH)
MERGED = (2 * WIDTH, 1024)
STRIPS, STRIP = 4, 48


def from_eight(blocks, which):
    return jnp.concatenate([blocks[peer, which] for peer in range(8)], axis=1)


def from_four(blocks, at=0):
    return jnp.concatenate(
        [blocks[chip, at + side] for chip in range(4) for side in range(2)], axis=1
    )


def pack_body(sides, coarse, packed, held, arrived, sent):
    arrays = [sides.at[1], sides.at[3], coarse.at[0]]
    loads = [
        [
            pltpu.make_async_copy(array.at[half], held.at[half, i], arrived.at[half, i])
            for i, array in enumerate(arrays)
        ]
        for half in range(2)
    ]
    for load in loads[0] + loads[1]:
        load.start()
    stores = []
    for half in range(2):
        for load in loads[half]:
            load.wait()
        for peer in range(half, 8, 2):
            store = pltpu.make_async_copy(held.at[half], packed.at[peer], sent.at[peer])
            store.start()
            stores.append(store)
    for store in stores:
        store.wait()


def pack(sides, coarse):
    return pl.pallas_call(
        pack_body,
        out_shape=pltpu.HBM((8, 3, HALF, WIDTH), BF16),
        in_specs=[HBM, HBM],
        out_specs=HBM,
        scratch_shapes=[
            pltpu.VMEM((2, 3, HALF, WIDTH), BF16),
            pltpu.SemaphoreType.DMA((2, 3)),
            pltpu.SemaphoreType.DMA((8,)),
        ],
        compiler_params=pltpu.CompilerParams(vmem_limit_bytes=4 << 20),
    )(
        pltpu.with_memory_space_constraint(sides, pltpu.HBM),
        pltpu.with_memory_space_constraint(coarse, pltpu.HBM),
    )


def own_and_partner(total):
    return total[:, :WIDTH], total[:, WIDTH:]


def spread(copies, results, at=0):
    mine = core()
    for chip in range(4):
        copies[chip, at + mine] = results[0]
        copies[chip, at + 1 - mine] = results[1]


def bundle_body(
    one, two, solve_one, solve_two, sides, coarse, first, second, lifts,
    first_held, held, lifts_held, arrived, sent,
):
    other = 1 - core()
    incoming, outgoing = Pieces(arrived), Pieces(sent)
    pair, triple = pl.ds(0, 2), pl.ds(2, 3)
    rows = []
    for j in range(3 * STRIPS):
        half = coarse.at[0, other] if j < STRIPS else sides.at[2 * (j // STRIPS - 1), other]
        strip = half.at[pl.ds(STRIP * (j % STRIPS), STRIP)]
        rows.append(incoming.load(strip, strip_of(first_held, j)))
    groups = (
        (one.at[1], first_held.at[pair], first.at[pair]),
        (one.at[0, 1], held.at[0], second.at[0]),
        (two.at[0, 1], held.at[1], second.at[1]),
        (solve_two.at[0], held.at[triple], second.at[triple]),
        (solve_one.at[0], held.at[pl.ds(5, 3)], second.at[pl.ds(5, 3)]),
        (solve_one.at[1], held.at[pl.ds(8, 3)], second.at[pl.ds(8, 3)]),
        (one.at[0, 0], lifts_held.at[0], lifts.at[0]),
        (two.at[0, 0], lifts_held.at[1], lifts.at[1]),
    )
    loads = [incoming.load(source, place) for source, place, _ in groups]
    for row in rows:
        row.wait()
    used = pl.ds(0, 2 * STRIP)
    outgoing.load(first_held.at[2, used], first.at[2, used])
    for load, (_, place, target) in zip(loads, groups):
        load.wait()
        outgoing.load(place, target)
    outgoing.wait()


def strip_of(bundle, j):
    row, column = (0, j) if j < 2 * STRIPS else (1, j - 2 * STRIPS)
    return bundle.at[2, pl.ds(STRIP * row, STRIP), pl.ds(WIDTH * column, WIDTH)]


def bundled(*arrays):
    shapes = [(3, WIDTH, 1024), (11, WIDTH, 1024), (2, WIDTH, 1024)]
    return pl.pallas_call(
        bundle_body,
        out_shape=[pltpu.HBM(shape, BF16) for shape in shapes],
        in_specs=[HBM] * len(arrays),
        out_specs=[HBM] * 3,
        scratch_shapes=[pltpu.VMEM(shape, BF16) for shape in shapes]
        + [
            pltpu.SemaphoreType.DMA((8 + 3 * STRIPS,)),
            pltpu.SemaphoreType.DMA((9,)),
        ],
        compiler_params=pltpu.CompilerParams(vmem_limit_bytes=12 << 20),
        cost_estimate=pl.CostEstimate(
            flops=0, bytes_accessed=9000000, transcendentals=0
        ),
    )(*[pltpu.with_memory_space_constraint(x, pltpu.HBM) for x in arrays])


def load_half(pieces, own, bundle, which, held):
    pieces.load(own, held.at[0])
    for j in range(STRIPS):
        place = held.at[1, pl.ds(STRIP * j, STRIP)]
        pieces.load(strip_of(bundle, STRIPS * which + j), place)


def prepare_body(one, sides, coarse, bundle, matrices, begun, coarse_pair, sems):
    pieces, mine = Pieces(sems), core()
    load_half(pieces, coarse.at[0, mine], bundle, 0, coarse_pair)
    for i in range(2):
        pieces.both(one.at[1, i], bundle.at[i], matrices.at[i])
    for i in range(2):
        load_half(pieces, sides.at[2 * i, mine], bundle, 1 + i, begun.at[i])
    pieces.wait()


def middle_body(odd, matrices, begun, following, copies, sems):
    total = apply(from_eight(odd, 0), matrices[0])
    total += apply(from_eight(odd, 1), matrices[1])
    spread(
        copies,
        [
            (begun[1, i].astype(F32) - part).astype(BF16)
            for i, part in enumerate(own_and_partner(total))
        ],
    )
    spread(copies, [following[0], following[1]], 2)


def early_body(
    odd, one, solve, last, bundle, inverses, coarse, early, onward, held, sems
):
    pieces = Pieces(sems)
    waits = [
        pieces.both(own, partner, held.at[i])
        for i, (own, partner) in enumerate(
            (
                (last.at[0, 1], bundle.at[3]),
                (solve.at[0, 0], bundle.at[5]),
                (solve.at[0, 1], bundle.at[6]),
                (solve.at[1, 0], bundle.at[8]),
                (one.at[0, 1], bundle.at[0]),
            )
        )
    ]
    rest = pieces.both(last.at[0, 0], bundle.at[2], inverses.at[0])
    rest += pieces.both(last.at[0, 2], bundle.at[4], inverses.at[1])

    def product(vector, i):
        for copy in waits[i]:
            copy.wait()
        return apply(vector, held[i])

    second, fourth, here = (from_eight(odd, i) for i in range(3))
    onward[...] = fourth
    coarse[...] = product(here, 0)
    early[0] = product(second, 1) - product(here, 2)
    early[1] = product(fourth, 3)
    early[2] = product(second, 4)
    for copy in rest:
        copy.wait()


def centre_body(gathered, inverses, coarse, copies, sems):
    total = apply(from_four(gathered), inverses[0])
    total -= apply(from_four(gathered, 2), inverses[1]) + coarse[...]
    spread(copies, [part.astype(BF16) for part in own_and_partner(total)])


def onward_body(
    gathered, fourth, lifts, lifts_partner, totals, held, fourth_held, sems
):
    pieces = Pieces(sems)
    for i in range(2):
        pieces.both(lifts.at[i], lifts_partner.at[i], held.at[i])
    pieces.load(fourth, fourth_held)
    full = from_four(gathered)
    pieces.wait()
    total = apply(fourth_held[...], held[0]) + apply(full, held[1])
    for i, part in enumerate(own_and_partner(total)):
        totals[i] = part.astype(BF16)


def reduced_body(
    gathered, early, two, solve, coarse, second, sides_begun,
    total, matrices, begun, kept, held, sides_held, early_held, sems,
):
    pieces = Pieces(sems)
    pieces.both(two.at[0, 1], second.at[1], held.at[0])
    pieces.both(solve.at[1, 2], second.at[10], held.at[1])
    pieces.load(early, early_held)
    pieces.load(sides_begun.at[0], sides_held)
    pieces.both(solve.at[0, 2], second.at[7], matrices.at[0])
    pieces.both(solve.at[1, 1], second.at[9], matrices.at[1])
    pieces.load(coarse.at[0], kept)
    pieces.wait()
    begun[0] = early_held[0]
    both = early_held[2] + apply(from_four(gathered), held[0])
    for i, part in enumerate(own_and_partner(both)):
        total[i] = sides_held[i].astype(F32) - part
    begun[1] = early_held[1] - apply(from_four(gathered, 2), held[1])


def final_body(centre, matrices, begun, total, before, kept, given, sems):
    full = from_four(centre)
    chip, mine = lax.div(lax.axis_index("col"), 2), core()
    first = begun[0] - apply(full, matrices[0])
    last = begun[1] - apply(full, matrices[1])
    for i, out in enumerate((kept, given)):
        out[0] = own_and_partner(first)[i].astype(BF16)
        out[1] = centre[chip, mine if i == 0 else 1 - mine]
        out[2] = own_and_partner(last)[i].astype(BF16)
        out[3] = (total[i] - before[i].astype(F32)).astype(BF16)


def place_body(taken, coarse, kept, solved, reduced, sems):
    mine = core()
    solved[0] = coarse[...]
    for i in range(3):
        solved[i + 1, mine] = kept[i]
        solved[i + 1, 1 - mine] = taken[1 - mine, i]
    reduced[0, mine] = kept[3]
    reduced[0, 1 - mine] = taken[1 - mine, 3]


def steps(right_sides, coarse_solution, lift_one, solve_one, lift_two, solve_two):
    sides = right_sides.reshape(4, 2, HALF, WIDTH)
    coarse = coarse_solution.reshape(1, 2, HALF, WIDTH)
    packed = pack(sides, coarse)
    odd = lax.all_to_all(packed, "col", 0, 0)
    first, second, lifts = bundled(
        lift_one, lift_two, solve_one, solve_two, sides, coarse
    )
    first = from_partner(first)
    second = from_partner(second)
    lift_matrices, begun, coarse_pair = call(
        prepare_body,
        [
            (IN_VMEM, (2, *MERGED), BF16),
            (IN_VMEM, (2, *PAIR), BF16),
            (IN_VMEM, PAIR, BF16),
        ],
        [],
        [lift_one, sides, coarse],
        free=[first],
        copies=19,
    )
    following = passed_along(coarse_pair, -1)
    lifts_next = passed_along(lifts, -1)
    lifts_partner = from_partner(lifts_next)
    (middle_copies,) = call(
        middle_body,
        [(IN_HBM, (4, 4, HALF, WIDTH), BF16)],
        [odd, lift_matrices, begun, following],
        products=2,
    )
    gathered = over_chips(middle_copies)
    flat = (HALF, 2 * WIDTH)
    inverses, coarse_begun, early, fourth = call(
        early_body,
        [
            (IN_VMEM, (2, *MERGED), BF16),
            (IN_VMEM, flat, F32),
            (IN_HBM, (3, *flat), F32),
            (IN_HBM, (HALF, 1024), BF16),
        ],
        [odd],
        [lift_one, solve_one, solve_two, second],
        [((5, *MERGED), BF16)],
        copies=14,
        products=5,
    )
    (centre_copies,) = call(
        centre_body,
        [(IN_HBM, COPIES, BF16)],
        [gathered, inverses, coarse_begun],
        products=2,
    )
    centre = over_chips(centre_copies)
    (onward,) = call(
        onward_body,
        [(IN_VMEM, PAIR, BF16)],
        [gathered],
        [fourth, lifts_next],
        [((2, *MERGED), BF16), ((HALF, 1024), BF16)],
        free=[lifts_partner],
        copies=5,
    )
    before = passed_along(onward, 1)
    total, solve_matrices, ends_begun, coarse_kept = call(
        reduced_body,
        [
            (IN_VMEM, PAIR, F32),
            (IN_VMEM, (2, *MERGED), BF16),
            (IN_VMEM, (2, *flat), F32),
            (IN_VMEM, PAIR, BF16),
        ],
        [gathered],
        [early, lift_two, solve_one, coarse, second],
        [((2, *MERGED), BF16), (PAIR, BF16), ((3, *flat), F32)],
        free=[begun],
        copies=11,
        products=3,
    )
    kept, given = call(
        final_body,
        [(IN_VMEM, (4, HALF, WIDTH), BF16)] * 2,
        [centre, solve_matrices, ends_begun, total, before],
        products=2,
    )
    cores = [[i, i + 1] for i in range(0, lax.axis_size("col"), 2)]
    taken = lax.all_gather(given, "col", axis=0, axis_index_groups=cores)
    solved, reduced = call(
        place_body,
        [
            (IN_HBM, (4, 2, HALF, WIDTH), BF16),
            (IN_HBM, (1, 2, HALF, WIDTH), BF16),
        ],
        [taken, coarse_kept, kept],
    )
    return solved.reshape(4, ROWS, WIDTH), reduced.reshape(1, ROWS, WIDTH)


def solution(mesh):
    return jax.shard_map(
        steps,
        mesh=mesh,
        in_specs=(
            P("rad", None, "col"),
            P("rad", None, "col"),
            P("rad", None, "col", None),
            P("rad", None, "col", None),
            P("rad", None, "col", None),
            P("rad", None, "col", None),
        ),
        out_specs=(P("rad", None, "col"), P("rad", None, "col")),
        check_vma=False,
    )
```
